512 devices in a mesh: ctx: 32 (over z_lo, y, core), dp: 16 (over x, z_hi).
Axes of the slice: x: 4, y: 8, z: 8 (z_hi: 4, z_lo: 2; z = z_hi * 2 + z_lo), core: 2. Of those that a mesh axis runs over, the one named last changes fastest.
Arguments:
- queries: bfloat16 [16, 8192, 1024], P('dp', 'ctx'), may hold values from -6 to 6
- key_vecs: bfloat16 [16, 8192, 1024], P('dp', 'ctx'), may hold values from -6 to 6
- value_vecs: bfloat16 [16, 8192, 1024], P('dp', 'ctx'), may hold values from -6 to 6
- out_grad: bfloat16 [16, 8192, 1024], P('dp', 'ctx'), may hold values from -6 to 6
- out_weight: bfloat16 [1024, 1024], P(('ctx', 'dp')), may hold values from -0.1875 to 0.1875
Outputs:
- query_grad: bfloat16 [16, 8192, 1024], P('dp', 'ctx')
- key_grad: bfloat16 [16, 8192, 1024], P('dp', 'ctx')
- value_grad: bfloat16 [16, 8192, 1024], P('dp', 'ctx')
- weight_grad: float32 [1024, 1024], P(('ctx', 'dp'))
The draws below stay inside these ranges and needn't reach their ends.
All inputs are finite; a program needn't handle non-finite values.
Results may differ from the reference program's by a relative error of at most 0.0057.
Values may be sent and summed in bfloat16 or wider, within the bound.
A program may use at most 128 MiB of HBM per device.

```python
import math
import jax
import jax.numpy as jnp
from jax import lax

D = 1024
HEADS = 8
HEAD = 128
BLOCK = 256
TOK_DEV = 256
SEQLEN = 8192
SEQS = 16
N_CTX = 32
N_DP = 16


def levels(stream_key, dims, shards, low, largest):
    gain = 1.0
    for position, blocks in shards:
        draws = jax.random.uniform(jax.random.fold_in(jax.random.fold_in(stream_key, 6), position), (blocks,), jnp.float32, low / len(shards), largest / len(shards))
        gain = gain * jnp.repeat(jnp.exp(draws), dims[position] // blocks).reshape((-1,) + (1,) * (len(dims) - 1 - position))
    return gain


def scatter_about(key, dims, spread, bound, pieces=(), kind=jnp.bfloat16):
    result = spread * jax.random.normal(key, dims, jnp.float32)
    if pieces:
        result = result * levels(key, dims, pieces, -0.22, 0.18)
    return jnp.clip(result, -bound, bound).astype(kind)


def setup_inputs(seed: int = 0) -> dict:
    streams_of = jax.random.split(jax.random.key(seed), 6)
    queries = scatter_about(streams_of[0], (SEQS, SEQLEN, HEADS * HEAD), 1.0, 6.0, ((0, 16), (1, 32)))
    key_vecs = scatter_about(streams_of[1], (SEQS, SEQLEN, HEADS * HEAD), 1.0, 6.0, ((0, 16), (1, 32)))
    value_vecs = scatter_about(streams_of[2], (SEQS, SEQLEN, HEADS * HEAD), 1.0, 6.0, ((0, 16), (1, 32)))
    out_grad = scatter_about(streams_of[3], (SEQS, SEQLEN, D), 1.0, 6.0, ((0, 16), (1, 32)))
    out_weight = scatter_about(streams_of[4], (HEADS * HEAD, D), D ** -0.5, 0.1875, ((0, 512),))
    return dict(queries=queries, key_vecs=key_vecs, value_vecs=value_vecs, out_grad=out_grad, out_weight=out_weight)


def ein(form, left, right):
    return jnp.einsum(form, left.astype(jnp.float32), right.astype(jnp.float32))

def sequence_grads(qry_rows, key_rows, val_rows, grd_rows, att_scale):
    width = qry_rows.shape[-1]
    count = qry_rows.shape[0] // BLOCK

    def split(array):
        return array.reshape(count, BLOCK, HEADS, HEAD)
    qry_blk = split(qry_rows)
    key_blk = split(key_rows)
    val_blk = split(val_rows)
    grd_blk = split(grd_rows)
    kv_block = ein('bshe,bshf->bhef', key_blk, val_blk)
    qd_block = ein('bthf,bthe->bhfe', grd_blk, qry_blk)
    state_in = (jnp.cumsum(kv_block, 0) - kv_block).astype(jnp.bfloat16)
    carried = (jnp.cumsum(qd_block[::-1], 0)[::-1] - qd_block).astype(jnp.bfloat16)
    positions = jnp.arange(BLOCK)
    causal = positions[:, None] >= positions[None, :]
    scores = jnp.where(causal, ein('bthe,bshe->bhts', qry_blk, key_blk), 0.0).astype(jnp.bfloat16)
    attended = att_scale * (ein('bhts,bshf->bthf', scores, val_blk) + ein('bthe,bhef->bthf', qry_blk, state_in))
    dscores = jnp.where(causal, ein('bthf,bshf->bhts', grd_blk, val_blk), 0.0).astype(jnp.bfloat16)
    query_grad = att_scale * (ein('bhts,bshe->bthe', dscores, key_blk) + ein('bthf,bhef->bthe', grd_blk, state_in))
    key_grad = att_scale * (ein('bhts,bthe->bshe', dscores, qry_blk) + ein('bshf,bhfe->bshe', val_blk, carried))
    value_grad = att_scale * (ein('bhts,bthf->bshf', scores, grd_blk) + ein('bshe,bhfe->bshf', key_blk, carried))
    return (attended.astype(jnp.bfloat16).reshape(-1, width), query_grad.astype(jnp.bfloat16).reshape(-1, width), key_grad.astype(jnp.bfloat16).reshape(-1, width), value_grad.astype(jnp.bfloat16).reshape(-1, width))

def reference(queries, key_vecs, value_vecs, out_grad, out_weight):
    att_scale = 1.0 / math.sqrt(HEAD * TOK_DEV * N_CTX)
    inv_root = 1.0 / math.sqrt(N_DP * TOK_DEV * N_CTX)
    width = HEADS * HEAD
    flat_grad = out_grad.reshape(-1, D)
    att_grad = jnp.dot(flat_grad, out_weight.T, preferred_element_type=jnp.float32).astype(jnp.bfloat16)
    att_grad = att_grad.reshape(queries.shape[0], queries.shape[1], width)

    def one_sequence(members):
        return sequence_grads(members[0], members[1], members[2], members[3], att_scale)
    attended, query_grad, key_grad, value_grad = lax.map(one_sequence, (queries, key_vecs, value_vecs, att_grad))
    weight_grad = jnp.dot(attended.reshape(-1, width).T, flat_grad, preferred_element_type=jnp.float32) * inv_root
    return (query_grad, key_grad, value_grad, weight_grad)
```

```python
import math

import jax
import jax.numpy as jnp
from jax import lax
from jax.experimental import pallas as pl
from jax.experimental.pallas import tpu as pltpu
from jax.sharding import PartitionSpec as P

HEAD = 128
HEADS = 8
TOK = 256
D = 1024
NX, NY, NZ = 4, 8, 8
NCTX = 32
F32, BF16 = jnp.float32, jnp.bfloat16
MESH = pl.DeviceIdType.MESH


def device(x, y, z, core):
    return (((z % 2) * NY + y) * 2 + core, x * (NZ // 2) + z // 2)


def dot(left, right, dims):
    return lax.dot_general(left, right, (dims, ((), ())), preferred_element_type=F32)


def tn(left, right):
    return dot(left, right, ((0,), (0,)))


def nt(left, right):
    return dot(left, right, ((1,), (1,)))


def nn(left, right):
    return dot(left, right, ((1,), (0,)))


def kernel(
    att_scale, inv_root,
    q_ref, k_ref, v_ref, g_ref, w_ref,
    dq_ref, dk_ref, dv_ref, wg_ref,
    tiles, weight, kv_out, kv_in, kv_sum, kv_back, qd_out, qd_in, qd_sum, qd_back,
    scores, dscores, acc, att_grad, dk_acc, dv_acc, attended,
    part, part_in, sum1, in1, sum2, in2, sum3, in3, flat,
    ag_s, ag_r, scan_s, scan_r, rs_s, rs_r,
):
    ctx, dp = lax.axis_index("ctx"), lax.axis_index("dp")
    core, y, zl = ctx % 2, (ctx // 2) % NY, ctx // (2 * NY)
    x, zh = dp // (NZ // 2), dp % (NZ // 2)
    z = zh * 2 + zl

    def at_y(o):
        return device(x, (y + o) % NY, z, core)

    def at_z(o):
        return device(x, y, (z + o) % NZ, core)

    def at_x(o):
        return device((x + o) % NX, y, z, core)

    other = device(x, y, z, 1 - core)

    def remote(src, dst, s, r, to):
        return pltpu.make_async_remote_copy(
            src_ref=src, dst_ref=dst, send_sem=s, recv_sem=r, device_id=to, device_id_type=MESH
        )

    barrier = pltpu.get_barrier_semaphore()

    def greet(o, carry):
        pl.semaphore_signal(barrier, inc=1, device_id=((ctx + o) % NCTX, dp), device_id_type=MESH)
        return carry

    lax.fori_loop(1, NCTX, greet, 0)
    for o in range(1, NX):
        pl.semaphore_signal(barrier, inc=1, device_id=at_x(o), device_id_type=MESH)
    for o in range(2, NZ):
        pl.semaphore_signal(
            barrier, inc=1, device_id=device(x, y, (z - zl + (zl + o) % 2 + (o - o % 2)) % NZ, core),
            device_id_type=MESH,
        )
    own = w_ref[...].astype(F32)
    for row in range(2):
        for cb in range(8):
            flat[row * 8 + cb : row * 8 + cb + 1, :] = own[row : row + 1, cb * 128 : cb * 128 + 128]
    tiles[zl, y, core, x, zh] = flat[...].astype(BF16)
    pl.semaphore_wait(barrier, NCTX - 1 + NX - 1 + NZ - 2)

    stage1 = [
        remote(tiles.at[zl, y, core, x, zh], tiles.at[zl, y, core, x, zh], ag_s.at[o - 1], ag_r.at[o - 1], at_y(o))
        for o in range(1, NY)
    ]
    for copy in stage1:
        copy.start()

    def exchange(src, dst, sems):
        def send(o, carry):
            to = (ctx + o) % NCTX
            remote(src.at[to], dst.at[ctx], scan_s.at[sems], scan_r.at[sems], (to, dp)).start()
            return carry

        lax.fori_loop(1, NCTX, send, 0)
        dst[ctx] = src[ctx]
        every = pl.ds(0, NCTX - 1)
        return remote(src.at[every], dst.at[every], scan_s.at[sems], scan_r.at[sems], other)

    for h in range(HEADS):
        cols = slice(h * HEAD, h * HEAD + HEAD)
        product = tn(k_ref[:, cols], v_ref[:, cols]).astype(BF16)
        kv_out[h * 4 : h * 4 + 4] = product.reshape(4, 32, HEAD)
    kv_there = exchange(kv_out, kv_in, 0)

    for copy in stage1:
        copy.wait_recv()
    column = tiles.at[zl, :, core, x, zh]
    stage2 = [
        remote(column, column, ag_s.at[6 + o], ag_r.at[6 + o], at_z(o)) for o in range(1, NZ)
    ]
    for copy in stage2:
        copy.start()

    causal = lax.broadcasted_iota(jnp.int32, (TOK, TOK), 0) >= lax.broadcasted_iota(jnp.int32, (TOK, TOK), 1)
    for h in range(HEADS):
        cols = slice(h * HEAD, h * HEAD + HEAD)
        masked = jnp.where(causal, nt(q_ref[:, cols], k_ref[:, cols]), 0.0).astype(BF16)
        scores[h] = masked
        acc[:, cols] = nn(masked, v_ref[:, cols])

    kv_there.wait_recv()
    total = jnp.zeros((32, HEAD), F32)
    for s in range(NCTX):
        kv_sum[s] = total.astype(BF16)
        total = total + kv_in[s].astype(F32)
    kv_home = exchange(kv_sum, kv_back, 1)

    for copy in stage2:
        copy.wait_recv()
    def plane(a):
        return tiles.at[:, :, core, a]

    stage3 = [
        remote(plane(x), plane(x), ag_s.at[13 + o], ag_r.at[13 + o], at_x(o)) for o in range(1, NX)
    ]
    for copy in stage3:
        copy.start()
    swaps = [
        remote(plane((x - o + NX) % NX), plane((x - o + NX) % NX), ag_s.at[17 + o], ag_r.at[17 + o], other)
        for o in range(NX)
    ]
    swaps[0].start()
    for o in range(1, NX):
        stage3[o - 1].wait_recv()
        swaps[o].start()

    rows_i = lax.broadcasted_iota(jnp.int32, (256, 256), 0)
    cols_i = lax.broadcasted_iota(jnp.int32, (256, 256), 1)

    def tile_row(i):
        return ((i & 31) >> 1) * 16 + (i & 1) * 8 + (i >> 5)

    to_rows = jnp.where(cols_i == tile_row(rows_i), 1.0, 0.0).astype(BF16)
    to_tiles = jnp.where(rows_i == tile_row(cols_i), 1.0, 0.0).astype(BF16)

    def place(which):
        def one(i, carry):
            a, b = i // NY, i % NY
            rows = nn(to_rows, tiles[a, b, which].reshape(256, 128)).astype(BF16)
            at = pl.ds(pl.multiple_of((i * 2 + which) * 32, 32), 32)
            for cb in range(8):
                weight[at, cb * 128 : cb * 128 + 128] = rows[cb * 32 : cb * 32 + 32]
            return carry

        lax.fori_loop(0, 16, one, 0)

    place(core)
    for copy in swaps:
        copy.wait_recv()
    place(1 - core)

    for h in range(HEADS):
        cols = slice(h * HEAD, h * HEAD + HEAD)
        grad = nt(g_ref[...], weight[cols, :]).astype(BF16)
        att_grad[:, cols] = grad
        product = tn(grad, q_ref[:, cols]).astype(BF16)
        qd_out[h * 4 : h * 4 + 4] = product.reshape(4, 32, HEAD)
    qd_there = exchange(qd_out, qd_in, 2)

    kv_home.wait_recv()
    pairs = []
    for h in range(HEADS):
        cols = slice(h * HEAD, h * HEAD + HEAD)
        state = kv_back[h * 4 : h * 4 + 4].reshape(HEAD, HEAD)
        mixed = (att_scale * (acc[:, cols] + nn(q_ref[:, cols], state))).astype(BF16)
        term = tn(mixed, g_ref[...]).astype(BF16)
        for b in range(4):
            rows = term[b * 32 : b * 32 + 32]
            stacked = jnp.concatenate([rows[:, cb * 128 : cb * 128 + 128] for cb in range(8)], 0)
            block = h * 4 + b
            part[block // 16, (block // 2) % 8, block % 2] = (
                nn(to_tiles, stacked).astype(BF16).reshape(NX, NZ // 2, 16, 128)
            )
        half = (h // 4, pl.ds((h % 4) * 2, 2))
        copy = remote(
            part.at[half[0], half[1], 1 - core], part_in.at[half[0], half[1]], rs_s.at[h], rs_r.at[h], other
        )
        copy.start()
        pairs.append(copy)

    for h in range(HEADS):
        cols = slice(h * HEAD, h * HEAD + HEAD)
        grad = att_grad[:, cols]
        masked = jnp.where(causal, nt(grad, v_ref[:, cols]), 0.0).astype(BF16)
        state = kv_back[h * 4 : h * 4 + 4].reshape(HEAD, HEAD)
        dq_ref[:, cols] = (att_scale * (nn(masked, k_ref[:, cols]) + nt(grad, state))).astype(BF16)
        dk_acc[:, cols] = tn(masked, q_ref[:, cols])
        dv_acc[:, cols] = tn(scores[h], grad)

    for h in range(HEADS):
        pairs[h].wait_recv()
        for b in range(2):
            a, row = h // 4, (h % 4) * 2 + b
            both = part[a, row, core].astype(F32) + part_in[a, row].astype(F32)
            sum1[:, :, a, row] = both.astype(BF16)
    by_x = []
    for o in range(1, NX):
        copy = remote(sum1.at[(x + o) % NX], in1.at[o - 1], rs_s.at[7 + o], rs_r.at[7 + o], at_x(o))
        copy.start()
        by_x.append(copy)

    qd_there.wait_recv()
    total = jnp.zeros((32, HEAD), F32)
    for s in reversed(range(NCTX)):
        qd_sum[s] = total.astype(BF16)
        total = total + qd_in[s].astype(F32)
    qd_home = exchange(qd_sum, qd_back, 3)

    for copy in by_x:
        copy.wait_recv()

    def add_x(i, carry):
        value = sum1[x, i // 2, i % 2].astype(F32)
        for o in range(NX - 1):
            value = value + in1[o, i // 2, i % 2].astype(F32)
        sum2[i] = value.astype(BF16)
        return carry

    lax.fori_loop(0, NZ, add_x, 0)
    by_z = []
    for o in range(1, NZ):
        copy = remote(sum2.at[(z + o) % NZ], in2.at[o - 1], rs_s.at[10 + o], rs_r.at[10 + o], at_z(o))
        copy.start()
        by_z.append(copy)

    qd_home.wait_recv()
    for h in range(HEADS):
        cols = slice(h * HEAD, h * HEAD + HEAD)
        carried = qd_back[h * 4 : h * 4 + 4].reshape(HEAD, HEAD)
        dk_ref[:, cols] = (att_scale * (dk_acc[:, cols] + nn(v_ref[:, cols], carried))).astype(BF16)
        dv_ref[:, cols] = (att_scale * (dv_acc[:, cols] + nt(k_ref[:, cols], carried))).astype(BF16)

    for copy in by_z:
        copy.wait_recv()
    value = sum2[z].astype(F32)
    for o in range(NZ - 1):
        value = value + in2[o].astype(F32)
    sum3[...] = value.astype(BF16)
    by_y = []
    for o in range(1, NY):
        copy = remote(sum3.at[(y + o) % NY], in3.at[o - 1], rs_s.at[17 + o], rs_r.at[17 + o], at_y(o))
        copy.start()
        by_y.append(copy)
    for copy in by_y:
        copy.wait_recv()
    value = sum3[y].astype(F32)
    for o in range(NY - 1):
        value = value + in3[o].astype(F32)
    value = value * inv_root
    for row in range(2):
        for cb in range(8):
            wg_ref[row : row + 1, cb * 128 : cb * 128 + 128] = value[row * 8 + cb : row * 8 + cb + 1, :]

    for copy in stage1 + stage2 + stage3 + swaps + pairs + by_x + by_z + by_y:
        copy.wait_send()
    for copy in (kv_there, kv_home, qd_there, qd_home):
        copy.wait_send()


def per_device(queries, key_vecs, value_vecs, out_grad, out_weight):
    att_scale = 1.0 / math.sqrt(HEAD * TOK * NCTX)
    inv_root = 1.0 / math.sqrt(16 * TOK * NCTX)

    def body(*refs):
        kernel(att_scale, inv_root, *refs)

    vmem = pl.BlockSpec(memory_space=pltpu.VMEM)
    piece = pltpu.VMEM((NCTX, 32, HEAD), BF16)
    wide = pltpu.VMEM((TOK, D), F32)
    narrow = pltpu.VMEM((TOK, D), BF16)
    out = jax.ShapeDtypeStruct((TOK, D), BF16)
    dq, dk, dv, wg = pl.pallas_call(
        body,
        out_shape=(out, out, out, jax.ShapeDtypeStruct((2, D), F32)),
        in_specs=[vmem] * 5,
        out_specs=(vmem,) * 4,
        scratch_shapes=[
            pltpu.VMEM((2, NY, 2, NX, NZ // 2, 16, 128), BF16),
            pltpu.VMEM((D, D), BF16),
            piece, piece, piece, piece, piece, piece, piece, piece,
            pltpu.VMEM((HEADS, TOK, TOK), BF16),
            pltpu.VMEM((8, 128), BF16),
            wide, narrow, wide, wide,
            pltpu.VMEM((8, 128), BF16),
            pltpu.VMEM((2, NY, 2, NX, NZ // 2, 16, 128), BF16),
            pltpu.VMEM((2, NY, NX, NZ // 2, 16, 128), BF16),
            pltpu.VMEM((NX, NZ // 2, 2, NY, 16, 128), BF16),
            pltpu.VMEM((NX - 1, NZ // 2, 2, NY, 16, 128), BF16),
            pltpu.VMEM((NZ, NY, 16, 128), BF16),
            pltpu.VMEM((NZ - 1, NY, 16, 128), BF16),
            pltpu.VMEM((NY, 16, 128), BF16),
            pltpu.VMEM((NY - 1, 16, 128), BF16),
            pltpu.VMEM((16, 128), F32),
            pltpu.SemaphoreType.DMA((21,)), pltpu.SemaphoreType.DMA((21,)),
            pltpu.SemaphoreType.DMA((4,)), pltpu.SemaphoreType.DMA((4,)),
            pltpu.SemaphoreType.DMA((25,)), pltpu.SemaphoreType.DMA((25,)),
        ],
        compiler_params=pltpu.CompilerParams(
            collective_id=0, has_side_effects=True, vmem_limit_bytes=48 << 20
        ),
        name="backward",
    )(queries[0], key_vecs[0], value_vecs[0], out_grad[0], out_weight)
    return dq[None], dk[None], dv[None], wg


def solution(mesh):
    rows = P("dp", "ctx", None)
    return jax.shard_map(
        per_device,
        mesh=mesh,
        in_specs=(rows, rows, rows, rows, P(("ctx", "dp"), None)),
        out_specs=(rows, rows, rows, P(("ctx", "dp"), None)),
        check_vma=False,
    )
```

```python
import math

import jax
import jax.numpy as jnp
from jax import lax
from jax.experimental import pallas as pl
from jax.experimental.pallas import tpu as pltpu
from jax.sharding import PartitionSpec as P

HEAD = 128
HEADS = 8
HALF = HEADS // 2
TOK = 256
D = 1024
NX, NY, NZ = 4, 8, 8
ZH = NZ // 2
CHIPS = 2 * NY
NCTX = 2 * CHIPS
F32, BF16 = jnp.float32, jnp.bfloat16
MESH = pl.DeviceIdType.MESH


def device(x, y, z, core):
    return (((z % 2) * NY + y) * 2 + core, x * ZH + z // 2)


def dot(left, right, dims):
    return lax.dot_general(left, right, (dims, ((), ())), preferred_element_type=F32)


def tn(left, right):
    return dot(left, right, ((0,), (0,)))


def nt(left, right):
    return dot(left, right, ((1,), (1,)))


def nn(left, right):
    return dot(left, right, ((1,), (0,)))


def head(h):
    return slice(h * HEAD, h * HEAD + HEAD)


def kernel(
    att_scale, inv_root,
    q_hbm, k_hbm, v_hbm, g_hbm, w_hbm,
    dq_ref, dk_ref, dv_ref, wg_ref,
    q, k, v, g, w, g_other, v_turned,
    tiles, weight, flat, to_rows, to_tiles,
    kv, kv_pair, kv_out, kv_in, kv_sum, kv_back, kv_give, state,
    qd, qd_pair, qd_out, qd_in, qd_sum, qd_back, qd_give, carried,
    scores, att_acc, att, att_in, att_grad, dk_acc, dv_acc,
    sum1, in1, sum2, in2, sum3, in3,
    in1a, in1b, sum2a, sum2b, in2a, in2b, sum3c, in3c,
    load_sem, ag_s, ag_r, pair_s, pair_r, scan_s, scan_r, rs_s, rs_r,
):
    ctx, dp = lax.axis_index("ctx"), lax.axis_index("dp")
    core, chip = ctx % 2, ctx // 2
    y, zl = chip % NY, chip // NY
    x, zh = dp // ZH, dp % ZH
    z = zh * 2 + zl
    mine, theirs = pl.ds(core * HALF, HALF), pl.ds((1 - core) * HALF, HALF)
    other = (chip * 2 + 1 - core, dp)

    def at_x(o):
        return device((x + o) % NX, y, z, core)

    def at_y(o):
        return device(x, (y + o) % NY, z, core)

    def at_z(o):
        return device(x, y, (z + o) % NZ, core)

    def remote(src, dst, s, r, to):
        return pltpu.make_async_remote_copy(
            src_ref=src, dst_ref=dst, send_sem=s, recv_sem=r, device_id=to, device_id_type=MESH
        )

    def by_core(of_core_0, of_core_1):
        pl.when(core == 0)(of_core_0)
        pl.when(core == 1)(of_core_1)

    sent, open_waits = [], {}

    def begin(name, make):
        for copy in make():
            copy.start()
        open_waits[name] = lambda: [copy.wait_recv() for copy in make()]
        sent.append(lambda: [copy.wait_send() for copy in make()])

    def begin_by_core(name, make_0, make_1):
        by_core(lambda: [copy.start() for copy in make_0()] and None, lambda: [copy.start() for copy in make_1()] and None)
        open_waits[name] = lambda: by_core(
            lambda: [copy.wait_recv() for copy in make_0()] and None,
            lambda: [copy.wait_recv() for copy in make_1()] and None,
        )
        sent.append(
            lambda: by_core(
                lambda: [copy.wait_send() for copy in make_0()] and None,
                lambda: [copy.wait_send() for copy in make_1()] and None,
            )
        )

    def wait(name):
        open_waits.pop(name)()

    loads = [
        pltpu.make_async_copy(src, dst, load_sem.at[i])
        for i, (src, dst) in enumerate(((k_hbm, k), (v_hbm, v), (w_hbm, w), (q_hbm, q), (g_hbm, g)))
    ]
    barrier = pltpu.get_barrier_semaphore()

    def enter():
        for load in loads:
            load.start()
        greeted = [((((chip + o) % CHIPS) * 2 + core), dp) for o in range(1, CHIPS)]
        greeted += [other]
        greeted += [at_x(o) for o in range(1, NX)]
        greeted += [
            device(x, y, (zh * 2 + 2 * (o // 2) + (zl + o) % 2) % NZ, core) for o in range(2, NZ)
        ]
        for to in greeted:
            pl.semaphore_signal(barrier, inc=1, device_id=to, device_id_type=MESH)
        loads[2].wait()
        own = w[...].astype(F32)
        for row in range(2):
            for cb in range(8):
                flat[row * 8 + cb : row * 8 + cb + 1, :] = own[row : row + 1, head(cb)]
        tiles[zl, y, core, x, zh] = flat[...].astype(BF16)
        pl.semaphore_wait(barrier, len(greeted))

    def products():
        loads[0].wait()
        loads[1].wait()
        for h in range(HEADS):
            turned = v[:, head(h)].T
            v_turned[head(h), :] = turned
            kv[h] = nn(turned, k[:, head(h)])

    def one_hot():
        rows_i = lax.broadcasted_iota(jnp.int32, (256, 256), 0)
        cols_i = lax.broadcasted_iota(jnp.int32, (256, 256), 1)

        def tile_row(i):
            return ((i & 31) >> 1) * 16 + (i & 1) * 8 + (i >> 5)

        to_rows[...] = jnp.where(cols_i == tile_row(rows_i), 1.0, 0.0).astype(BF16)
        to_tiles[...] = jnp.where(rows_i == tile_row(cols_i), 1.0, 0.0).astype(BF16)

    def ring(ref, first, to, n):
        return [remote(ref, ref, ag_s.at[first + o], ag_r.at[first + o], to(o)) for o in range(1, n)]

    def gather1_0():
        return ring(tiles.at[zl, y, 0, x, zh], 0, at_y, NY)

    def gather1_1():
        return ring(tiles.at[zl, y, 1, x, zh], 0, at_x, NX)

    def gather2_0():
        return ring(tiles.at[zl, :, 0, x, zh], 8, at_z, NZ)

    def gather2_1():
        return ring(tiles.at[zl, y, 1, 0:2, zh], 8, at_y, NY) + ring(tiles.at[zl, y, 1, 2:4, zh], 16, at_z, NZ)

    def gather3_0():
        return ring(tiles.at[:, :, 0, x], 24, at_x, NX)

    def gather3_1():
        return ring(tiles.at[zl, :, 1, 0:2, zh], 24, at_z, NZ) + ring(tiles.at[:, y, 1, 2:4], 32, at_y, NY)

    def swap_refs_0():
        return [tiles.at[:, :, 0, (x - o + NX) % NX] for o in range(NX)]

    def swap_refs_1():
        refs = []
        for o in range(NZ):
            far = (z - o + NZ) % NZ
            refs.append(tiles.at[far % 2, :, 1, 0:2, far // 2])
        return refs + [tiles.at[:, (y - o + NY) % NY, 1, 2:4] for o in range(NY)]

    def swap(refs):
        return [remote(ref, ref, ag_s.at[40 + i], ag_r.at[40 + i], other) for i, ref in enumerate(refs)]

    def hand_over():
        def go(arriving, refs, own):
            copies = swap(refs)
            for i in own:
                copies[i].start()
            for copy, i in arriving:
                copy.wait_recv()
                copies[i].start()

        def go_0():
            go(zip(gather3_0(), range(1, NX)), swap_refs_0(), [0])

        def go_1():
            order = list(zip(gather3_1(), list(range(1, NZ)) + list(range(NZ + 1, NZ + NY))))
            both = [p for pair in zip(order[: NZ - 1], order[NZ - 1 :]) for p in pair]
            go(both, swap_refs_1(), [0, NZ])

        open_waits.pop("gather3")
        by_core(go_0, go_1)
        open_waits["swap"] = lambda: by_core(
            lambda: [copy.wait_recv() for copy in swap(swap_refs_1())] and None,
            lambda: [copy.wait_recv() for copy in swap(swap_refs_0())] and None,
        )
        sent.append(
            lambda: by_core(
                lambda: [copy.wait_send() for copy in swap(swap_refs_0())] and None,
                lambda: [copy.wait_send() for copy in swap(swap_refs_1())] and None,
            )
        )

    def place(which):
        def one(b, carry):
            both = jnp.concatenate([tiles[a, b, which].reshape(256, 128) for a in range(2)], 1)
            rows = nn(to_rows[...], both).astype(BF16)
            for a in range(2):
                at = pl.ds(pl.multiple_of(((a * NY + b) * 2 + which) * 32, 32), 32)
                for cb in range(8):
                    weight[at, cb * 128 : cb * 128 + 128] = rows[cb * 32 : cb * 32 + 32, a * 128 : a * 128 + 128]
            return carry

        lax.fori_loop(0, NY, one, 0)

    def pair(src, dst, i):
        return lambda: [remote(src, dst, pair_s.at[i], pair_r.at[i], other)]

    def exchange(src, dst, i):
        def make():
            copies = []
            for o in range(1, CHIPS):
                to = (chip + o) % CHIPS
                copies.append(
                    remote(src.at[to], dst.at[chip], scan_s.at[i, o], scan_r.at[i, o], (to * 2 + core, dp))
                )
            return copies

        return make

    def add_pair(product, received, out):
        for h in range(HALF):
            both = product[core * HALF + h] + received[h]
            out[h * 4 : h * 4 + 4] = both.astype(BF16).reshape(4, 32, HEAD)

    def running(received, out, order):
        total = jnp.zeros((32, HEAD), F32)
        for s in order:
            out[s] = total.astype(BF16)
            total = total + received[s].astype(F32)

    def finish(product, received, back, give, out, core_behind):
        for h in range(HALF):
            base = back[h * 4 : h * 4 + 4].reshape(HEAD, HEAD).astype(F32)
            keep = jnp.where(core == core_behind, base + received[h], base)
            hand = jnp.where(core == core_behind, base, base + product[core * HALF + h])
            out[core * HALF + h] = keep.astype(BF16)
            give[h] = hand.astype(BF16)

    def spread(src, dst, first, to, n):
        return [remote(src(o), dst.at[o - 1], rs_s.at[first + o], rs_r.at[first + o], to(o)) for o in range(1, n)]

    def far_z(o):
        return (z + o) % NZ

    def far_y(o):
        return (y + o) % NY

    def scatter1_0(a, half):
        rows = pl.ds(half * 4, 4)
        copies = []
        for o in range(1, NX):
            i = (a * 2 + half) * NX + o
            copies.append(
                remote(
                    sum1.at[(x + o) % NX, :, a, rows], in1.at[o - 1, :, a, rows], rs_s.at[i], rs_r.at[i], at_x(o)
                )
            )
        return copies

    def scatter1_z(o, half):
        rows, far = pl.ds(half * 4, 4), (z + o) % NZ
        i = half * NZ + o
        return remote(
            sum1.at[0:2, far // 2, far % 2, rows], in1a.at[o - 1, :, rows], rs_s.at[i], rs_r.at[i], at_z(o)
        )

    def scatter1_y(o):
        i = 2 * NZ + o
        return remote(sum1.at[2:4, :, :, (y + o) % NY], in1b.at[o - 1], rs_s.at[i], rs_r.at[i], at_y(o))

    def scatter1(a, half):
        def of_core_0():
            for copy in scatter1_0(a, half):
                copy.start()

        def of_core_1():
            for far in range(ZH):
                o = (far * 2 + a - z + NZ) % NZ

                @pl.when(o != 0)
                def _():
                    scatter1_z(o, half).start()

            if a == 1:
                for far in range(4):
                    o = (half * 4 + far - y + NY) % NY

                    @pl.when(o != 0)
                    def _():
                        scatter1_y(o).start()

        by_core(of_core_0, of_core_1)

    def scatter1_all(act):
        def of_core_0():
            for half in range(2):
                for a in range(2):
                    for copy in scatter1_0(a, half):
                        act(copy)

        def of_core_1():
            for half in range(2):
                for o in range(1, NZ):
                    act(scatter1_z(o, half))
            for o in range(1, NY):
                act(scatter1_y(o))

        by_core(of_core_0, of_core_1)

    def scatter2_0():
        return spread(lambda o: sum2.at[far_z(o)], in2, 24, at_z, NZ)

    def scatter2_1():
        return spread(lambda o: sum2a.at[:, far_y(o)], in2a, 24, at_y, NY) + spread(
            lambda o: sum2b.at[:, far_z(o) // 2, far_z(o) % 2], in2b, 32, at_z, NZ
        )

    def scatter3_0():
        return spread(lambda o: sum3.at[far_y(o)], in3, 40, at_y, NY)

    def scatter3_1():
        return spread(lambda o: sum3c.at[(x + o) % NX], in3c, 40, at_x, NX)

    def total_of(own, received):
        value = own.astype(F32)
        for i in range(received.shape[0]):
            value = value + received[i].astype(F32)
        return value

    causal_t = lax.broadcasted_iota(jnp.int32, (TOK, TOK), 1) >= lax.broadcasted_iota(jnp.int32, (TOK, TOK), 0)

    def begin_all():
        begin_by_core("gather1", gather1_0, gather1_1)
        products()
        begin("kv pair", pair(kv.at[theirs], kv_pair, 0))
        loads[3].wait()
        loads[4].wait()
        begin("out_grad", pair(g, g_other, 1))
        one_hot()

    def kv_there():
        wait("kv pair")
        add_pair(kv, kv_pair, kv_out)
        begin("kv there", exchange(kv_out, kv_in, 0))
        kv_in[chip] = kv_out[chip]

    def second_gather():
        wait("gather1")
        begin_by_core("gather2", gather2_0, gather2_1)

    def score():
        for h in range(HEADS):
            masked = jnp.where(causal_t, nt(k[:, head(h)], q[:, head(h)]), 0.0).astype(BF16)
            scores[h] = masked
            att_acc[head(h), :] = nn(v_turned[head(h), :], masked)

    def third_gather():
        wait("gather2")
        begin_by_core("gather3", gather3_0, gather3_1)

    def kv_home():
        wait("kv there")
        running(kv_in, kv_sum, range(CHIPS))
        begin("kv home", exchange(kv_sum, kv_back, 1))
        kv_back[chip] = kv_sum[chip]

    def states():
        wait("kv home")
        finish(kv, kv_pair, kv_back, kv_give, state, 1)
        begin("states", pair(kv_give, state.at[mine], 2))

    def attend():
        wait("states")
        for h in range(HEADS):
            mixed = att_scale * (att_acc[head(h), :] + nt(state[h], q[:, head(h)]))
            att[2 * h : 2 * h + 2] = mixed.astype(BF16).reshape(2, 2, 32, TOK)
        begin("attended", pair(att.at[:, 1 - core], att_in, 3))

    def terms():
        wait("out_grad")
        wait("attended")
        for half, a in ((0, 0), (0, 1), (1, 0), (1, 1)):
            first = a * NY + half * 4
            blocks = slice(first, first + 4)
            left = att[blocks, core].reshape(128, TOK)
            right = att_in[blocks].reshape(128, TOK)
            term = (nn(left, g[...]) + nn(right, g_other[...])).astype(BF16)
            for j in range(2):
                both = jnp.concatenate(
                    [
                        jnp.concatenate(
                            [term[b * 32 : b * 32 + 32, head(cb)] for cb in range(8)], 0
                        )
                        for b in (2 * j, 2 * j + 1)
                    ],
                    1,
                )
                units = nn(to_tiles[...], both).astype(BF16)
                for b in range(2):
                    sum1[:, :, a, half * 4 + 2 * j + b] = units[:, head(b)].reshape(NX, ZH, 16, 128)
            scatter1(a, half)
        open_waits["scatter1"] = lambda: scatter1_all(lambda copy: copy.wait_recv())
        sent.append(lambda: scatter1_all(lambda copy: copy.wait_send()))

    def own_weights():
        place(core)

    def other_weights():
        wait("swap")
        place(1 - core)

    def qd_pairs():
        for i in range(4):
            rows = slice(i * 256, i * 256 + 256)
            grad = nt(weight[rows, :], g[...]).astype(BF16)
            att_grad[rows, :] = grad
            for h in range(2):
                qd[2 * i + h] = nn(grad[head(h)], q[:, head(2 * i + h)])
        begin("qd pair", pair(qd.at[theirs], qd_pair, 4))

    def qd_there():
        wait("qd pair")
        add_pair(qd, qd_pair, qd_out)
        begin("qd there", exchange(qd_out, qd_in, 2))
        qd_in[chip] = qd_out[chip]

    def local_grads():
        for h in range(HEADS):
            grad = att_grad[head(h), :]
            masked = jnp.where(causal_t, nn(v[:, head(h)], grad), 0.0).astype(BF16)
            dq_ref[:, head(h)] = (att_scale * (tn(masked, k[:, head(h)]) + tn(grad, state[h]))).astype(BF16)
            dk_acc[:, head(h)] = nn(masked, q[:, head(h)])
            dv_acc[:, head(h)] = nt(scores[h], grad)

    def second_scatter():
        wait("scatter1")

        def sum_0():
            def one(i, carry):
                value = sum1[x, i // 2, i % 2].astype(F32)
                for o in range(NX - 1):
                    value = value + in1[o, i // 2, i % 2].astype(F32)
                sum2[i] = value.astype(BF16)
                return carry

            lax.fori_loop(0, NZ, one, 0)

        def sum_1():
            sum2a[...] = total_of(sum1[0:2, zh, zl], in1a).astype(BF16)
            sum2b[...] = total_of(sum1[2:4, :, :, y], in1b).astype(BF16)

        by_core(sum_0, sum_1)
        begin_by_core("scatter2", scatter2_0, scatter2_1)

    def qd_home():
        wait("qd there")
        running(qd_in, qd_sum, reversed(range(CHIPS)))
        begin("qd home", exchange(qd_sum, qd_back, 3))
        qd_back[chip] = qd_sum[chip]

    def third_scatter():
        wait("scatter2")

        def sum_0():
            sum3[...] = total_of(sum2[z], in2)

        def sum_1():
            sum3c[0:2] = total_of(sum2a[:, y], in2a)
            sum3c[2:4] = total_of(sum2b[:, zh, zl], in2b)

        by_core(sum_0, sum_1)
        begin_by_core("scatter3", scatter3_0, scatter3_1)

    def laters():
        wait("qd home")
        finish(qd, qd_pair, qd_back, qd_give, carried, 0)
        begin("carried", pair(qd_give, carried.at[mine], 5))

    def weight_grad():
        wait("scatter3")

        def write(value):
            value = value * inv_root
            for row in range(2):
                for cb in range(8):
                    wg_ref[row : row + 1, head(cb)] = value[row * 8 + cb : row * 8 + cb + 1, :]

        by_core(lambda: write(total_of(sum3[y], in3)), lambda: write(total_of(sum3c[x], in3c)))

    def last_grads():
        wait("carried")
        for h in range(HEADS):
            dk_ref[:, head(h)] = (att_scale * (dk_acc[:, head(h)] + nn(v[:, head(h)], carried[h]))).astype(BF16)
            dv_ref[:, head(h)] = (att_scale * (dv_acc[:, head(h)] + nt(k[:, head(h)], carried[h]))).astype(BF16)

    steps = [
        enter, begin_all, kv_there, second_gather, score, third_gather, kv_home,
        hand_over, states, own_weights, attend, other_weights, qd_pairs, terms, qd_there, local_grads,
        second_scatter, qd_home, third_scatter, laters, weight_grad, last_grads,
    ]
    for step in steps:
        step()
    for name in list(open_waits):
        wait(name)
    for done in sent:
        done()


def store(*refs):
    sems = refs[8]
    copies = [pltpu.make_async_copy(refs[i], refs[4 + i], sems.at[i]) for i in range(4)]
    for copy in copies:
        copy.start()
    for copy in copies:
        copy.wait()


def per_device(queries, key_vecs, value_vecs, out_grad, out_weight):
    att_scale = 1.0 / math.sqrt(HEAD * TOK * NCTX)
    inv_root = 1.0 / math.sqrt(16 * TOK * NCTX)

    def body(*refs):
        kernel(att_scale, inv_root, *refs)

    hbm = pl.BlockSpec(memory_space=pltpu.HBM)
    vmem = pl.BlockSpec(memory_space=pltpu.VMEM)
    wide, narrow = pltpu.VMEM((TOK, D), F32), pltpu.VMEM((TOK, D), BF16)
    piece = pltpu.VMEM((CHIPS, 32, HEAD), BF16)
    scan = [
        pltpu.VMEM((HEADS, HEAD, HEAD), F32), pltpu.VMEM((HALF, HEAD, HEAD), F32),
        piece, piece, piece, piece,
        pltpu.VMEM((HALF, HEAD, HEAD), BF16), pltpu.VMEM((HEADS, HEAD, HEAD), BF16),
    ]
    unit = (16, 128)

    def units(*dims, kind=BF16):
        return pltpu.VMEM(dims + unit, kind)

    out = jax.ShapeDtypeStruct((TOK, D), BF16)
    dq, dk, dv, wg = pl.pallas_call(
        body,
        out_shape=(out, out, out, jax.ShapeDtypeStruct((2, D), F32)),
        in_specs=[hbm] * 5,
        out_specs=(vmem,) * 4,
        scratch_shapes=[
            narrow, narrow, narrow, narrow, pltpu.VMEM((2, D), BF16), narrow, pltpu.VMEM((D, TOK), BF16),
            units(2, NY, 2, NX, ZH), pltpu.VMEM((D, D), BF16), pltpu.VMEM(unit, F32),
            pltpu.VMEM((256, 256), BF16), pltpu.VMEM((256, 256), BF16),
            *scan, *scan,
            pltpu.VMEM((HEADS, TOK, TOK), BF16), pltpu.VMEM((D, TOK), F32),
            pltpu.VMEM((CHIPS, 2, 32, TOK), BF16), pltpu.VMEM((CHIPS, 32, TOK), BF16), pltpu.VMEM((D, TOK), BF16), wide, wide,
            units(NX, ZH, 2, NY), units(NX - 1, ZH, 2, NY),
            units(NZ, NY), units(NZ - 1, NY), units(NY, kind=F32), units(NY - 1, kind=F32),
            units(NZ - 1, 2, NY), units(NY - 1, 2, ZH, 2), units(2, NY), units(2, ZH, 2),
            units(NY - 1, 2), units(NZ - 1, 2), units(NX, kind=F32), units(NX - 1, kind=F32),
            pltpu.SemaphoreType.DMA((5,)),
            pltpu.SemaphoreType.DMA((56,)), pltpu.SemaphoreType.DMA((56,)),
            pltpu.SemaphoreType.DMA((6,)), pltpu.SemaphoreType.DMA((6,)),
            pltpu.SemaphoreType.DMA((4, CHIPS)), pltpu.SemaphoreType.DMA((4, CHIPS)),
            pltpu.SemaphoreType.DMA((48,)), pltpu.SemaphoreType.DMA((48,)),
        ],
        compiler_params=pltpu.CompilerParams(
            collective_id=0, has_side_effects=True, vmem_limit_bytes=(62 << 20) + (256 << 10)
        ),
        name="backward",
    )(queries[0], key_vecs[0], value_vecs[0], out_grad[0], out_weight)
    dq, dk, dv, wg = pl.pallas_call(
        store,
        out_shape=(out, out, out, jax.ShapeDtypeStruct((2, D), F32)),
        in_specs=[hbm] * 4,
        out_specs=(hbm,) * 4,
        scratch_shapes=[pltpu.SemaphoreType.DMA((4,))],
        name="store",
    )(dq, dk, dv, wg)
    return dq[None], dk[None], dv[None], wg


def solution(mesh):
    rows = P("dp", "ctx", None)
    return jax.shard_map(
        per_device,
        mesh=mesh,
        in_specs=(rows, rows, rows, rows, P(("ctx", "dp"), None)),
        out_specs=(rows, rows, rows, P(("ctx", "dp"), None)),
        check_vma=False,
    )
```

```python
import math

import jax
import jax.numpy as jnp
from jax import lax
from jax.experimental import pallas as pl
from jax.experimental.pallas import tpu as pltpu
from jax.sharding import PartitionSpec as P

HEAD = 128
HEADS = 8
HALF = HEADS // 2
TOK = 256
D = 1024
NX, NY, NZ = 4, 8, 8
ZH = NZ // 2
CHIPS = 2 * NY
NCTX = 2 * CHIPS
F32, BF16 = jnp.float32, jnp.bfloat16
MESH = pl.DeviceIdType.MESH


def device(x, y, z, core):
    return (((z % 2) * NY + y) * 2 + core, x * ZH + z // 2)


def dot(left, right, dims):
    return lax.dot_general(left, right, (dims, ((), ())), preferred_element_type=F32)


def tn(left, right):
    return dot(left, right, ((0,), (0,)))


def nt(left, right):
    return dot(left, right, ((1,), (1,)))


def nn(left, right):
    return dot(left, right, ((1,), (0,)))


def head(h):
    return slice(h * HEAD, h * HEAD + HEAD)


def kernel(
    att_scale, inv_root,
    q_hbm, k_hbm, v_hbm, g_hbm, w_hbm,
    dq_ref, dk_ref, dv_ref, wg_ref,
    q, k, v, g_both, w, v_turned,
    tiles, weight, flat, to_rows, to_tiles,
    kv, kv_pair, kv_out, kv_in, kv_sum, kv_back, kv_give, state,
    qd, qd_pair, qd_out, qd_in, qd_sum, qd_back, qd_give, carried,
    scores, att_acc, att, att_in, att_grad, dk_acc, dv_acc,
    sum1, in1, sum2, in2, sum3, in3,
    in1a, in1b, sum2a, sum2b, in2a, in2b, sum3c, in3c,
    load_sem, ag_s, ag_r, pair_s, pair_r, scan_s, scan_r, rs_s, rs_r,
):
    ctx, dp = lax.axis_index("ctx"), lax.axis_index("dp")
    core, chip = ctx % 2, ctx // 2
    y, zl = chip % NY, chip // NY
    x, zh = dp // ZH, dp % ZH
    z = zh * 2 + zl
    mine, theirs = pl.ds(core * HALF, HALF), pl.ds((1 - core) * HALF, HALF)
    other = (chip * 2 + 1 - core, dp)

    def at_x(o):
        return device((x + o) % NX, y, z, core)

    def at_y(o):
        return device(x, (y + o) % NY, z, core)

    def at_z(o):
        return device(x, y, (z + o) % NZ, core)

    def remote(src, dst, s, r, to):
        return pltpu.make_async_remote_copy(
            src_ref=src, dst_ref=dst, send_sem=s, recv_sem=r, device_id=to, device_id_type=MESH
        )

    def by_core(of_core_0, of_core_1):
        pl.when(core == 0)(of_core_0)
        pl.when(core == 1)(of_core_1)

    sent, open_waits = [], {}

    def begin(name, make):
        for copy in make():
            copy.start()
        open_waits[name] = lambda: [copy.wait_recv() for copy in make()]
        sent.append(lambda: [copy.wait_send() for copy in make()])

    def begin_by_core(name, make_0, make_1):
        by_core(lambda: [copy.start() for copy in make_0()] and None, lambda: [copy.start() for copy in make_1()] and None)
        open_waits[name] = lambda: by_core(
            lambda: [copy.wait_recv() for copy in make_0()] and None,
            lambda: [copy.wait_recv() for copy in make_1()] and None,
        )
        sent.append(
            lambda: by_core(
                lambda: [copy.wait_send() for copy in make_0()] and None,
                lambda: [copy.wait_send() for copy in make_1()] and None,
            )
        )

    def wait(name):
        open_waits.pop(name)()

    g, g_other = g_both.at[0:TOK], g_both.at[TOK : 2 * TOK]

    loads = [
        pltpu.make_async_copy(src, dst, load_sem.at[i])
        for i, (src, dst) in enumerate(((k_hbm, k), (v_hbm, v), (w_hbm, w), (q_hbm, q), (g_hbm, g)))
    ]
    barrier = pltpu.get_barrier_semaphore()

    def enter():
        for load in loads:
            load.start()
        greeted = [((((chip + o) % CHIPS) * 2 + core), dp) for o in range(1, CHIPS)]
        greeted += [other]
        greeted += [at_x(o) for o in range(1, NX)]
        greeted += [
            device(x, y, (zh * 2 + 2 * (o // 2) + (zl + o) % 2) % NZ, core) for o in range(2, NZ)
        ]
        for to in greeted:
            pl.semaphore_signal(barrier, inc=1, device_id=to, device_id_type=MESH)
        loads[2].wait()
        own = w[...].astype(F32)
        for row in range(2):
            for cb in range(8):
                flat[row * 8 + cb : row * 8 + cb + 1, :] = own[row : row + 1, head(cb)]
        tiles[zl, y, core, x, zh] = flat[...].astype(BF16)
        pl.semaphore_wait(barrier, len(greeted))

    def products():
        loads[0].wait()
        loads[1].wait()
        for h in range(HEADS):
            turned = v[:, head(h)].T
            v_turned[head(h), :] = turned
            kv[h] = nn(turned, k[:, head(h)])

    def one_hot():
        rows_i = lax.broadcasted_iota(jnp.int32, (256, 256), 0)
        cols_i = lax.broadcasted_iota(jnp.int32, (256, 256), 1)

        def tile_row(i):
            return ((i & 31) >> 1) * 16 + (i & 1) * 8 + (i >> 5)

        to_rows[...] = jnp.where(cols_i == tile_row(rows_i), 1.0, 0.0).astype(BF16)
        to_tiles[...] = jnp.where(rows_i == tile_row(cols_i), 1.0, 0.0).astype(BF16)

    def ring(ref, first, to, n):
        return [remote(ref, ref, ag_s.at[first + o], ag_r.at[first + o], to(o)) for o in range(1, n)]

    def gather1_0():
        return ring(tiles.at[zl, y, 0, x, zh], 0, at_y, NY)

    def gather1_1():
        return ring(tiles.at[zl, y, 1, x, zh], 0, at_x, NX)

    def gather2_0():
        return ring(tiles.at[zl, :, 0, x, zh], 8, at_z, NZ)

    def gather2_1():
        return ring(tiles.at[zl, y, 1, 0:2, zh], 8, at_y, NY) + ring(tiles.at[zl, y, 1, 2:4, zh], 16, at_z, NZ)

    def gather3_0():
        return ring(tiles.at[:, :, 0, x], 24, at_x, NX)

    def gather3_1():
        return ring(tiles.at[zl, :, 1, 0:2, zh], 24, at_z, NZ) + ring(tiles.at[:, y, 1, 2:4], 32, at_y, NY)

    def swap_refs_0():
        return [tiles.at[:, :, 0, (x - o + NX) % NX] for o in range(NX)]

    def swap_refs_1():
        refs = []
        for o in range(NZ):
            far = (z - o + NZ) % NZ
            refs.append(tiles.at[far % 2, :, 1, 0:2, far // 2])
        return refs + [tiles.at[:, (y - o + NY) % NY, 1, 2:4] for o in range(NY)]

    def swap(refs):
        return [remote(ref, ref, ag_s.at[40 + i], ag_r.at[40 + i], other) for i, ref in enumerate(refs)]

    def hand_over():
        def go(arriving, refs, own):
            copies = swap(refs)
            for i in own:
                copies[i].start()
            for copy, i in arriving:
                copy.wait_recv()
                copies[i].start()

        def go_0():
            go(zip(gather3_0(), range(1, NX)), swap_refs_0(), [0])

        def go_1():
            order = list(zip(gather3_1(), list(range(1, NZ)) + list(range(NZ + 1, NZ + NY))))
            both = [p for pair in zip(order[: NZ - 1], order[NZ - 1 :]) for p in pair]
            go(both, swap_refs_1(), [0, NZ])

        open_waits.pop("gather3")
        by_core(go_0, go_1)
        open_waits["swap"] = lambda: by_core(
            lambda: [copy.wait_recv() for copy in swap(swap_refs_1())] and None,
            lambda: [copy.wait_recv() for copy in swap(swap_refs_0())] and None,
        )
        sent.append(
            lambda: by_core(
                lambda: [copy.wait_send() for copy in swap(swap_refs_0())] and None,
                lambda: [copy.wait_send() for copy in swap(swap_refs_1())] and None,
            )
        )

    def place(which):
        def one(b, carry):
            both = jnp.concatenate([tiles[a, b, which].reshape(256, 128) for a in range(2)], 1)
            rows = nn(to_rows[...], both).astype(BF16)
            for a in range(2):
                at = pl.ds(pl.multiple_of(((a * NY + b) * 2 + which) * 32, 32), 32)
                for cb in range(8):
                    weight[at, cb * 128 : cb * 128 + 128] = rows[cb * 32 : cb * 32 + 32, a * 128 : a * 128 + 128]
            return carry

        lax.fori_loop(0, NY, one, 0)

    def pair(src, dst, i):
        return lambda: [remote(src, dst, pair_s.at[i], pair_r.at[i], other)]

    def exchange(src, dst, i):
        def make():
            copies = []
            for o in range(1, CHIPS):
                to = (chip + o) % CHIPS
                copies.append(
                    remote(src.at[to], dst.at[chip], scan_s.at[i, o], scan_r.at[i, o], (to * 2 + core, dp))
                )
            return copies

        return make

    def add_pair(product, received, out):
        for h in range(HALF):
            both = product[core * HALF + h] + received[h]
            out[h * 4 : h * 4 + 4] = both.astype(BF16).reshape(4, 32, HEAD)

    def running(received, out, order):
        total = jnp.zeros((32, HEAD), F32)
        for s in order:
            out[s] = total.astype(BF16)
            total = total + received[s].astype(F32)

    def finish(product, received, back, give, out, core_behind):
        for h in range(HALF):
            base = back[h * 4 : h * 4 + 4].reshape(HEAD, HEAD).astype(F32)
            keep = jnp.where(core == core_behind, base + received[h], base)
            hand = jnp.where(core == core_behind, base, base + product[core * HALF + h])
            out[core * HALF + h] = keep.astype(BF16)
            give[h] = hand.astype(BF16)

    def spread(src, dst, first, to, n):
        return [remote(src(o), dst.at[o - 1], rs_s.at[first + o], rs_r.at[first + o], to(o)) for o in range(1, n)]

    def far_z(o):
        return (z + o) % NZ

    def far_y(o):
        return (y + o) % NY

    def scatter1_0(a, half):
        rows = pl.ds(half * 4, 4)
        copies = []
        for o in range(1, NX):
            i = (a * 2 + half) * NX + o
            copies.append(
                remote(
                    sum1.at[(x + o) % NX, :, a, rows], in1.at[o - 1, :, a, rows], rs_s.at[i], rs_r.at[i], at_x(o)
                )
            )
        return copies

    def scatter1_z(o, half):
        rows, far = pl.ds(half * 4, 4), (z + o) % NZ
        i = half * NZ + o
        return remote(
            sum1.at[0:2, far // 2, far % 2, rows], in1a.at[o - 1, :, rows], rs_s.at[i], rs_r.at[i], at_z(o)
        )

    def scatter1_y(o):
        i = 2 * NZ + o
        return remote(sum1.at[2:4, :, :, (y + o) % NY], in1b.at[o - 1], rs_s.at[i], rs_r.at[i], at_y(o))

    def scatter1(turn):
        def of_core_0():
            for copy in scatter1_0(turn // 2, turn % 2):
                copy.start()

        def of_core_1():
            a, half = turn % 2, turn // 2
            for far in range(ZH):
                o = (far * 2 + a - z + NZ) % NZ

                @pl.when(o != 0)
                def _():
                    scatter1_z(o, half).start()

            if a == 1:
                for far in range(4):
                    o = (half * 4 + far - y + NY) % NY

                    @pl.when(o != 0)
                    def _():
                        scatter1_y(o).start()

        by_core(of_core_0, of_core_1)

    def scatter1_all(act):
        def of_core_0():
            for half in range(2):
                for a in range(2):
                    for copy in scatter1_0(a, half):
                        act(copy)

        def of_core_1():
            for half in range(2):
                for o in range(1, NZ):
                    act(scatter1_z(o, half))
            for o in range(1, NY):
                act(scatter1_y(o))

        by_core(of_core_0, of_core_1)

    def scatter2_z0(o):
        far = (z + o) % NZ
        return remote(sum2.at[far], in2.at[o - 1], rs_s.at[24 + o], rs_r.at[24 + o], at_z(o))

    def scatter2_y1(o):
        far = (y + o) % NY
        return remote(sum2a.at[:, far], in2a.at[o - 1], rs_s.at[24 + o], rs_r.at[24 + o], at_y(o))

    def scatter2_z1(o):
        far = (z + o) % NZ
        return remote(
            sum2b.at[:, far // 2, far % 2], in2b.at[o - 1], rs_s.at[32 + o], rs_r.at[32 + o], at_z(o)
        )

    def scatter2_all(act):
        def of_core_0():
            for o in range(1, NZ):
                act(scatter2_z0(o))

        def of_core_1():
            for o in range(1, NY):
                act(scatter2_y1(o))
            for o in range(1, NZ):
                act(scatter2_z1(o))

        by_core(of_core_0, of_core_1)

    def scatter3_0():
        return spread(lambda o: sum3.at[far_y(o)], in3, 40, at_y, NY)

    def scatter3_1():
        return spread(lambda o: sum3c.at[(x + o) % NX], in3c, 40, at_x, NX)

    def total_of(own, received):
        value = own.astype(F32)
        for i in range(received.shape[0]):
            value = value + received[i].astype(F32)
        return value

    causal_t = lax.broadcasted_iota(jnp.int32, (TOK, TOK), 1) >= lax.broadcasted_iota(jnp.int32, (TOK, TOK), 0)

    def begin_all():
        begin_by_core("gather1", gather1_0, gather1_1)
        products()
        begin("kv pair", pair(kv.at[theirs], kv_pair, 0))
        loads[3].wait()
        loads[4].wait()
        begin("out_grad", pair(g, g_other, 1))
        one_hot()

    def kv_there():
        wait("kv pair")
        add_pair(kv, kv_pair, kv_out)
        begin("kv there", exchange(kv_out, kv_in, 0))
        kv_in[chip] = kv_out[chip]

    def second_gather():
        wait("gather1")
        begin_by_core("gather2", gather2_0, gather2_1)

    def score():
        for h in range(HEADS):
            masked = jnp.where(causal_t, nt(k[:, head(h)], q[:, head(h)]), 0.0).astype(BF16)
            scores[h] = masked
            att_acc[head(h), :] = nn(v_turned[head(h), :], masked)

    def third_gather():
        wait("gather2")
        begin_by_core("gather3", gather3_0, gather3_1)

    def kv_home():
        wait("kv there")
        running(kv_in, kv_sum, range(CHIPS))
        begin("kv home", exchange(kv_sum, kv_back, 1))
        kv_back[chip] = kv_sum[chip]

    def states():
        wait("kv home")
        finish(kv, kv_pair, kv_back, kv_give, state, 1)
        begin("states", pair(kv_give, state.at[mine], 2))

    def attend():
        wait("states")
        for h in range(HEADS):
            mixed = att_scale * (att_acc[head(h), :] + nt(state[h], q[:, head(h)]))
            att[2 * h : 2 * h + 2] = mixed.astype(BF16).reshape(2, 2, 32, TOK)
        begin("attended", pair(att.at[:, 1 - core], att_in, 3))

    def terms():
        wait("out_grad")
        wait("attended")
        for turn in range(4):
            a = (1 - core) * (turn // 2) + core * (turn % 2)
            half = (1 - core) * (turn % 2) + core * (turn // 2)
            blocks = pl.ds(a * NY + half * 4, 4)
            left = jnp.concatenate(
                [att[blocks, core].reshape(128, TOK), att_in[blocks].reshape(128, TOK)], 1
            )
            term = nn(left, g_both[...]).astype(BF16)
            for j in range(2):
                both = jnp.concatenate(
                    [
                        jnp.concatenate(
                            [term[b * 32 : b * 32 + 32, head(cb)] for cb in range(8)], 0
                        )
                        for b in (2 * j, 2 * j + 1)
                    ],
                    1,
                )
                units = nn(to_tiles[...], both).astype(BF16)
                for b in range(2):
                    sum1[:, :, a, half * 4 + 2 * j + b] = units[:, head(b)].reshape(NX, ZH, 16, 128)
            scatter1(turn)
        sent.append(lambda: scatter1_all(lambda copy: copy.wait_send()))

    def own_weights():
        place(core)

    def other_weights():
        wait("swap")
        place(1 - core)

    def qd_pairs():
        def of_half(which):
            for i in range(2):
                rows = pl.ds(pl.multiple_of((which * 2 + i) * 256, 256), 256)
                grad = nt(weight[rows, :], g[...]).astype(BF16)
                att_grad[rows, :] = grad
                for j in range(2):
                    h = which * HALF + 2 * i + j
                    qd[h] = nn(grad[head(j)], q[:, pl.ds(pl.multiple_of(h * HEAD, HEAD), HEAD)])

        of_half(1 - core)
        begin("qd pair", pair(qd.at[theirs], qd_pair, 4))
        of_half(core)

    def qd_there():
        wait("qd pair")
        add_pair(qd, qd_pair, qd_out)
        begin("qd there", exchange(qd_out, qd_in, 2))
        qd_in[chip] = qd_out[chip]

    def local_grads():
        for h in range(HEADS):
            grad = att_grad[head(h), :]
            masked = jnp.where(causal_t, nn(v[:, head(h)], grad), 0.0).astype(BF16)
            dq_ref[:, head(h)] = (att_scale * (tn(masked, k[:, head(h)]) + tn(grad, state[h]))).astype(BF16)
            dk_acc[:, head(h)] = nn(masked, q[:, head(h)])
            dv_acc[:, head(h)] = nt(scores[h], grad)

    def second_scatter(part):
        def of_core_0():
            for half in range(2):
                for copy in scatter1_0(part, half):
                    copy.wait_recv()
            for far in range(ZH):
                value = sum1[x, far, part].astype(F32)
                for o in range(NX - 1):
                    value = value + in1[o, far, part].astype(F32)
                sum2[far * 2 + part] = value.astype(BF16)
                o = (far * 2 + part - z + NZ) % NZ

                @pl.when(o != 0)
                def _():
                    scatter2_z0(o).start()

        def of_core_1():
            rows = slice(part * 4, part * 4 + 4)
            for o in range(1, NZ):
                scatter1_z(o, part).wait_recv()
            value = sum1[0:2, zh, zl, rows].astype(F32)
            for o in range(NZ - 1):
                value = value + in1a[o, :, rows].astype(F32)
            sum2a[:, rows] = value.astype(BF16)
            for far in range(4):
                o = (part * 4 + far - y + NY) % NY

                @pl.when(o != 0)
                def _():
                    scatter2_y1(o).start()

            if part == 1:
                for o in range(1, NY):
                    scatter1_y(o).wait_recv()
                sum2b[...] = total_of(sum1[2:4, :, :, y], in1b).astype(BF16)
                for o in range(1, NZ):
                    scatter2_z1(o).start()

        by_core(of_core_0, of_core_1)
        if part == 1:
            open_waits["scatter2"] = lambda: scatter2_all(lambda copy: copy.wait_recv())
            sent.append(lambda: scatter2_all(lambda copy: copy.wait_send()))

    def second_scatter_0():
        second_scatter(0)

    def second_scatter_1():
        second_scatter(1)

    def qd_home():
        wait("qd there")
        running(qd_in, qd_sum, reversed(range(CHIPS)))
        begin("qd home", exchange(qd_sum, qd_back, 3))
        qd_back[chip] = qd_sum[chip]

    def third_scatter():
        wait("scatter2")

        def sum_0():
            sum3[...] = total_of(sum2[z], in2)

        def sum_1():
            sum3c[0:2] = total_of(sum2a[:, y], in2a)
            sum3c[2:4] = total_of(sum2b[:, zh, zl], in2b)

        by_core(sum_0, sum_1)
        begin_by_core("scatter3", scatter3_0, scatter3_1)

    def laters():
        wait("qd home")
        finish(qd, qd_pair, qd_back, qd_give, carried, 0)
        begin("carried", pair(qd_give, carried.at[mine], 5))

    def weight_grad():
        wait("scatter3")

        def write(value):
            value = value * inv_root
            for row in range(2):
                for cb in range(8):
                    wg_ref[row : row + 1, head(cb)] = value[row * 8 + cb : row * 8 + cb + 1, :]

        by_core(lambda: write(total_of(sum3[y], in3)), lambda: write(total_of(sum3c[x], in3c)))

    def last_grads():
        wait("carried")
        for h in range(HEADS):
            dk_ref[:, head(h)] = (att_scale * (dk_acc[:, head(h)] + nn(v[:, head(h)], carried[h]))).astype(BF16)
            dv_ref[:, head(h)] = (att_scale * (dv_acc[:, head(h)] + nt(k[:, head(h)], carried[h]))).astype(BF16)

    steps = [
        enter, begin_all, kv_there, second_gather, score, third_gather, kv_home,
        hand_over, states, own_weights, attend, other_weights, qd_pairs, qd_there, terms, local_grads,
        second_scatter_0, second_scatter_1, qd_home, third_scatter, laters, weight_grad, last_grads,
    ]
    for step in steps:
        step()
    for name in list(open_waits):
        wait(name)
    for done in sent:
        done()


def store(*refs):
    sems = refs[8]
    copies = [pltpu.make_async_copy(refs[i], refs[4 + i], sems.at[i]) for i in range(4)]
    for copy in copies:
        copy.start()
    for copy in copies:
        copy.wait()


def per_device(queries, key_vecs, value_vecs, out_grad, out_weight):
    att_scale = 1.0 / math.sqrt(HEAD * TOK * NCTX)
    inv_root = 1.0 / math.sqrt(16 * TOK * NCTX)

    def body(*refs):
        kernel(att_scale, inv_root, *refs)

    hbm = pl.BlockSpec(memory_space=pltpu.HBM)
    vmem = pl.BlockSpec(memory_space=pltpu.VMEM)
    wide, narrow = pltpu.VMEM((TOK, D), F32), pltpu.VMEM((TOK, D), BF16)
    piece = pltpu.VMEM((CHIPS, 32, HEAD), BF16)
    scan = [
        pltpu.VMEM((HEADS, HEAD, HEAD), F32), pltpu.VMEM((HALF, HEAD, HEAD), F32),
        piece, piece, piece, piece,
        pltpu.VMEM((HALF, HEAD, HEAD), BF16), pltpu.VMEM((HEADS, HEAD, HEAD), BF16),
    ]
    unit = (16, 128)

    def units(*dims, kind=BF16):
        return pltpu.VMEM(dims + unit, kind)

    out = jax.ShapeDtypeStruct((TOK, D), BF16)
    dq, dk, dv, wg = pl.pallas_call(
        body,
        out_shape=(out, out, out, jax.ShapeDtypeStruct((2, D), F32)),
        in_specs=[hbm] * 5,
        out_specs=(vmem,) * 4,
        scratch_shapes=[
            narrow, narrow, narrow, pltpu.VMEM((2 * TOK, D), BF16), pltpu.VMEM((2, D), BF16), pltpu.VMEM((D, TOK), BF16),
            units(2, NY, 2, NX, ZH), pltpu.VMEM((D, D), BF16), pltpu.VMEM(unit, F32),
            pltpu.VMEM((256, 256), BF16), pltpu.VMEM((256, 256), BF16),
            *scan, *scan,
            pltpu.VMEM((HEADS, TOK, TOK), BF16), pltpu.VMEM((D, TOK), F32),
            pltpu.VMEM((CHIPS, 2, 32, TOK), BF16), pltpu.VMEM((CHIPS, 32, TOK), BF16), pltpu.VMEM((D, TOK), BF16), wide, wide,
            units(NX, ZH, 2, NY), units(NX - 1, ZH, 2, NY),
            units(NZ, NY), units(NZ - 1, NY), units(NY, kind=F32), units(NY - 1, kind=F32),
            units(NZ - 1, 2, NY), units(NY - 1, 2, ZH, 2), units(2, NY), units(2, ZH, 2),
            units(NY - 1, 2), units(NZ - 1, 2), units(NX, kind=F32), units(NX - 1, kind=F32),
            pltpu.SemaphoreType.DMA((5,)),
            pltpu.SemaphoreType.DMA((56,)), pltpu.SemaphoreType.DMA((56,)),
            pltpu.SemaphoreType.DMA((6,)), pltpu.SemaphoreType.DMA((6,)),
            pltpu.SemaphoreType.DMA((4, CHIPS)), pltpu.SemaphoreType.DMA((4, CHIPS)),
            pltpu.SemaphoreType.DMA((48,)), pltpu.SemaphoreType.DMA((48,)),
        ],
        compiler_params=pltpu.CompilerParams(
            collective_id=0, has_side_effects=True, vmem_limit_bytes=48 << 20
        ),
        name="backward",
    )(*(pltpu.with_memory_space_constraint(a, pltpu.HBM) for a in (queries[0], key_vecs[0], value_vecs[0], out_grad[0], out_weight)))
    dq, dk, dv, wg = pl.pallas_call(
        store,
        out_shape=(out, out, out, jax.ShapeDtypeStruct((2, D), F32)),
        in_specs=[vmem] * 4,
        out_specs=(hbm,) * 4,
        scratch_shapes=[pltpu.SemaphoreType.DMA((4,))],
        name="store",
    )(*(pltpu.with_memory_space_constraint(a, pltpu.VMEM) for a in (dq, dk, dv, wg)))
    return dq[None], dk[None], dv[None], wg


def solution(mesh):
    rows = P("dp", "ctx", None)
    return jax.shard_map(
        per_device,
        mesh=mesh,
        in_specs=(rows, rows, rows, rows, P(("ctx", "dp"), None)),
        out_specs=(rows, rows, rows, P(("ctx", "dp"), None)),
        check_vma=False,
    )
```

```python
import math

import jax
import jax.numpy as jnp
from jax import lax
from jax.experimental import pallas as pl
from jax.experimental.pallas import tpu as pltpu
from jax.sharding import PartitionSpec as P

HEAD = 128
HEADS = 8
HALF = HEADS // 2
TOK = 256
D = 1024
NX, NY, NZ = 4, 8, 8
ZH = NZ // 2
CHIPS = 2 * NY
NCTX = 2 * CHIPS
F32, BF16 = jnp.float32, jnp.bfloat16
MESH = pl.DeviceIdType.MESH


def device(x, y, z, core):
    return (((z % 2) * NY + y) * 2 + core, x * ZH + z // 2)


def dot(left, right, dims):
    return lax.dot_general(left, right, (dims, ((), ())), preferred_element_type=F32)


def tn(left, right):
    return dot(left, right, ((0,), (0,)))


def nt(left, right):
    return dot(left, right, ((1,), (1,)))


def nn(left, right):
    return dot(left, right, ((1,), (0,)))


def head(h):
    return slice(h * HEAD, h * HEAD + HEAD)


def kernel(
    att_scale, inv_root,
    q_hbm, k_hbm, v_hbm, g_hbm, w_hbm,
    dq_ref, dk_ref, dv_ref, wg_ref,
    q, k, v, g_both, w, v_turned, q_other,
    tiles, weight, flat, to_rows, to_tiles,
    kv, kv_pair, kv_out, kv_in, kv_sum, kv_back, kv_give, state,
    qd_own, qd_other, qd_out, qd_in, qd_sum, qd_back, qd_give, carried,
    scores, att_acc, att, att_in, att_grad, grad_give, dk_acc, dv_acc,
    sum1, in1, sum2, in2, sum3, in3,
    in1a, in1b, sum2a, sum2b, in2a, in2b, sum3c, in3c,
    load_sem, ag_s, ag_r, pair_s, pair_r, scan_s, scan_r, rs_s, rs_r,
):
    ctx, dp = lax.axis_index("ctx"), lax.axis_index("dp")
    core, chip = ctx % 2, ctx // 2
    y, zl = chip % NY, chip // NY
    x, zh = dp // ZH, dp % ZH
    z = zh * 2 + zl
    mine, theirs = pl.ds(core * HALF, HALF), pl.ds((1 - core) * HALF, HALF)
    other = (chip * 2 + 1 - core, dp)

    def at_x(o):
        return device((x + o) % NX, y, z, core)

    def at_y(o):
        return device(x, (y + o) % NY, z, core)

    def at_z(o):
        return device(x, y, (z + o) % NZ, core)

    def remote(src, dst, s, r, to):
        return pltpu.make_async_remote_copy(
            src_ref=src, dst_ref=dst, send_sem=s, recv_sem=r, device_id=to, device_id_type=MESH
        )

    def by_core(of_core_0, of_core_1):
        pl.when(core == 0)(of_core_0)
        pl.when(core == 1)(of_core_1)

    sent, open_waits = [], {}

    def begin(name, make):
        for copy in make():
            copy.start()
        open_waits[name] = lambda: [copy.wait_recv() for copy in make()]
        sent.append(lambda: [copy.wait_send() for copy in make()])

    def begin_by_core(name, make_0, make_1):
        by_core(lambda: [copy.start() for copy in make_0()] and None, lambda: [copy.start() for copy in make_1()] and None)
        open_waits[name] = lambda: by_core(
            lambda: [copy.wait_recv() for copy in make_0()] and None,
            lambda: [copy.wait_recv() for copy in make_1()] and None,
        )
        sent.append(
            lambda: by_core(
                lambda: [copy.wait_send() for copy in make_0()] and None,
                lambda: [copy.wait_send() for copy in make_1()] and None,
            )
        )

    def wait(name):
        open_waits.pop(name)()

    g, g_other = g_both.at[0:TOK], g_both.at[TOK : 2 * TOK]

    loads = [
        pltpu.make_async_copy(src, dst, load_sem.at[i])
        for i, (src, dst) in enumerate(((w_hbm, w), (k_hbm, k), (v_hbm, v), (q_hbm, q), (g_hbm, g)))
    ]
    barrier = pltpu.get_barrier_semaphore()

    def enter():
        for load in loads:
            load.start()
        greeted = [((((chip + o) % CHIPS) * 2 + core), dp) for o in range(1, CHIPS)]
        greeted += [other]
        greeted += [at_x(o) for o in range(1, NX)]
        greeted += [
            device(x, y, (zh * 2 + 2 * (o // 2) + (zl + o) % 2) % NZ, core) for o in range(2, NZ)
        ]
        for to in greeted:
            pl.semaphore_signal(barrier, inc=1, device_id=to, device_id_type=MESH)
        loads[0].wait()
        own = w[...].astype(F32)
        for row in range(2):
            for cb in range(8):
                flat[row * 8 + cb : row * 8 + cb + 1, :] = own[row : row + 1, head(cb)]
        tiles[zl, y, core, x, zh] = flat[...].astype(BF16)
        pl.semaphore_wait(barrier, len(greeted))

    def products(which):
        for i in range(HALF):
            h = which * HALF + i
            cols = pl.ds(pl.multiple_of(h * HEAD, HEAD), HEAD)
            turned = v[:, cols].T
            v_turned[cols, :] = turned
            kv[h] = nn(turned, k[:, cols])

    def one_hot():
        rows_i = lax.broadcasted_iota(jnp.int32, (256, 256), 0)
        cols_i = lax.broadcasted_iota(jnp.int32, (256, 256), 1)

        def tile_row(i):
            return ((i & 31) >> 1) * 16 + (i & 1) * 8 + (i >> 5)

        to_rows[...] = jnp.where(cols_i == tile_row(rows_i), 1.0, 0.0).astype(BF16)
        to_tiles[...] = jnp.where(rows_i == tile_row(cols_i), 1.0, 0.0).astype(BF16)

    def ring(ref, first, to, n):
        return [remote(ref, ref, ag_s.at[first + o], ag_r.at[first + o], to(o)) for o in range(1, n)]

    def gather1_0():
        return ring(tiles.at[zl, y, 0, x, zh], 0, at_y, NY)

    def gather1_1():
        return ring(tiles.at[zl, y, 1, x, zh], 0, at_x, NX)

    def gather2_0():
        return ring(tiles.at[zl, :, 0, x, zh], 8, at_z, NZ)

    def gather2_1y():
        return ring(tiles.at[zl, y, 1, 0:2, zh], 8, at_y, NY)

    def gather2_1z():
        return ring(tiles.at[zl, y, 1, 2:4, zh], 16, at_z, NZ)

    def gather3_0(o):
        far = (z - o + NZ) % NZ
        return ring(tiles.at[far % 2, :, 0, x, far // 2], 24 + o * NX, at_x, NX)

    def gather3_1z():
        return ring(tiles.at[zl, :, 1, 0:2, zh], 24, at_z, NZ)

    def gather3_1y():
        return ring(tiles.at[:, y, 1, 2:4], 32, at_y, NY)

    def gather3_0_all():
        return [copy for o in range(NZ) for copy in gather3_0(o)]

    def start(copies):
        for copy in copies:
            copy.start()

    def second_gather():
        wait("gather1")

        def of_core_0():
            start(gather2_0())
            start(gather3_0(0))

        def of_core_1():
            start(gather2_1y())
            start(gather2_1z())

        by_core(of_core_0, of_core_1)

    def third_gather():
        def of_core_0():
            copies = gather2_0()
            for o in (1, 7, 2, 6, 3, 5, 4):
                copies[o - 1].wait_recv()
                start(gather3_0(o))

        def of_core_1():
            for copy in gather2_1y():
                copy.wait_recv()
            start(gather3_1z())
            for copy in gather2_1z():
                copy.wait_recv()
            start(gather3_1y())

        by_core(of_core_0, of_core_1)

        def all_of(last_only, act):
            def of_core_0():
                for copy in gather3_0_all() + ([] if last_only else gather2_0()):
                    act(copy)

            def of_core_1():
                for copy in gather3_1z() + gather3_1y() + ([] if last_only else gather2_1y() + gather2_1z()):
                    act(copy)

            by_core(of_core_0, of_core_1)

        open_waits["gather3"] = lambda: all_of(True, lambda copy: copy.wait_recv())
        sent.append(lambda: all_of(False, lambda copy: copy.wait_send()))

    def place():
        for b in range(NY):
            both = jnp.concatenate([tiles[a, b, core].reshape(256, 128) for a in range(2)], 1)
            rows = nn(to_rows[...], both).astype(BF16)
            for a in range(2):
                at = (a * NY + b) * 32
                for cb in range(8):
                    weight[at : at + 32, head(cb)] = rows[cb * 32 : cb * 32 + 32, head(a)]

    def pair(src, dst, i):
        return lambda: [remote(src, dst, pair_s.at[i], pair_r.at[i], other)]

    def exchange(src, dst, i):
        def make():
            copies = []
            for o in range(1, CHIPS):
                to = (chip + o) % CHIPS
                copies.append(
                    remote(src.at[to], dst.at[chip], scan_s.at[i, o], scan_r.at[i, o], (to * 2 + core, dp))
                )
            return copies

        return make

    def add_pair(product, received, out):
        for h in range(HALF):
            both = product[core * HALF + h] + received[h]
            out[h * 4 : h * 4 + 4] = both.astype(BF16).reshape(4, 32, HEAD)

    def running(received, out, order):
        total = jnp.zeros((32, HEAD), F32)
        for s in order:
            out[s] = total.astype(BF16)
            total = total + received[s].astype(F32)

    def finish():
        for h in range(HALF):
            base = kv_back[h * 4 : h * 4 + 4].reshape(HEAD, HEAD).astype(F32)
            state[core * HALF + h] = jnp.where(core == 1, base + kv_pair[h], base).astype(BF16)
            kv_give[h] = jnp.where(core == 1, base, base + kv[core * HALF + h]).astype(BF16)

    def spread(src, dst, first, to, n):
        return [remote(src(o), dst.at[o - 1], rs_s.at[first + o], rs_r.at[first + o], to(o)) for o in range(1, n)]

    def far_z(o):
        return (z + o) % NZ

    def far_y(o):
        return (y + o) % NY

    def scatter1_0(a, half):
        rows = pl.ds(half * 4, 4)
        copies = []
        for o in range(1, NX):
            i = (a * 2 + half) * NX + o
            copies.append(
                remote(
                    sum1.at[(x + o) % NX, :, a, rows], in1.at[o - 1, :, a, rows], rs_s.at[i], rs_r.at[i], at_x(o)
                )
            )
        return copies

    def scatter1_z(o, half):
        rows, far = pl.ds(half * 4, 4), (z + o) % NZ
        i = half * NZ + o
        return remote(
            sum1.at[0:2, far // 2, far % 2, rows], in1a.at[o - 1, :, rows], rs_s.at[i], rs_r.at[i], at_z(o)
        )

    def scatter1_y(o):
        i = 2 * NZ + o
        return remote(sum1.at[2:4, :, :, (y + o) % NY], in1b.at[o - 1], rs_s.at[i], rs_r.at[i], at_y(o))

    def scatter1(turn):
        def of_core_0():
            for copy in scatter1_0(turn // 2, turn % 2):
                copy.start()

        def of_core_1():
            a, half = turn % 2, turn // 2
            for far in range(ZH):
                o = (far * 2 + a - z + NZ) % NZ

                @pl.when(o != 0)
                def _():
                    scatter1_z(o, half).start()

            if a == 1:
                for far in range(4):
                    o = (half * 4 + far - y + NY) % NY

                    @pl.when(o != 0)
                    def _():
                        scatter1_y(o).start()

        by_core(of_core_0, of_core_1)

    def scatter1_all(act):
        def of_core_0():
            for half in range(2):
                for a in range(2):
                    for copy in scatter1_0(a, half):
                        act(copy)

        def of_core_1():
            for half in range(2):
                for o in range(1, NZ):
                    act(scatter1_z(o, half))
            for o in range(1, NY):
                act(scatter1_y(o))

        by_core(of_core_0, of_core_1)

    def scatter2_z0(o):
        far = (z + o) % NZ
        return remote(sum2.at[far], in2.at[o - 1], rs_s.at[24 + o], rs_r.at[24 + o], at_z(o))

    def scatter2_y1(o):
        far = (y + o) % NY
        return remote(sum2a.at[:, far], in2a.at[o - 1], rs_s.at[24 + o], rs_r.at[24 + o], at_y(o))

    def scatter2_z1(o):
        far = (z + o) % NZ
        return remote(
            sum2b.at[:, far // 2, far % 2], in2b.at[o - 1], rs_s.at[32 + o], rs_r.at[32 + o], at_z(o)
        )

    def scatter2_all(act):
        def of_core_0():
            for o in range(1, NZ):
                act(scatter2_z0(o))

        def of_core_1():
            for o in range(1, NY):
                act(scatter2_y1(o))
            for o in range(1, NZ):
                act(scatter2_z1(o))

        by_core(of_core_0, of_core_1)

    def scatter3_0():
        return spread(lambda o: sum3.at[far_y(o)], in3, 40, at_y, NY)

    def scatter3_1():
        return spread(lambda o: sum3c.at[(x + o) % NX], in3c, 40, at_x, NX)

    def total_of(own, received):
        value = own.astype(F32)
        for i in range(received.shape[0]):
            value = value + received[i].astype(F32)
        return value

    causal_t = lax.broadcasted_iota(jnp.int32, (TOK, TOK), 1) >= lax.broadcasted_iota(jnp.int32, (TOK, TOK), 0)

    def begin_all():
        begin_by_core("gather1", gather1_0, gather1_1)
        loads[1].wait()
        loads[2].wait()
        products(1 - core)
        begin("kv pair", pair(kv.at[theirs], kv_pair, 0))
        products(core)
        loads[3].wait()
        loads[4].wait()
        begin("out_grad", pair(g, g_other, 1))
        begin("queries", pair(q, q_other, 4))

    def kv_there():
        wait("kv pair")
        add_pair(kv, kv_pair, kv_out)
        begin("kv there", exchange(kv_out, kv_in, 0))
        kv_in[chip] = kv_out[chip]

    def score():
        for h in range(HEADS):
            masked = jnp.where(causal_t, nt(k[:, head(h)], q[:, head(h)]), 0.0).astype(BF16)
            scores[h] = masked
            att_acc[head(h), :] = nn(v_turned[head(h), :], masked)

    def kv_home():
        wait("kv there")
        running(kv_in, kv_sum, range(CHIPS))
        begin("kv home", exchange(kv_sum, kv_back, 1))
        kv_back[chip] = kv_sum[chip]
        one_hot()

    def states():
        wait("kv home")
        finish()
        begin("states", pair(kv_give, state.at[mine], 2))

    def attend():
        wait("states")
        for h in range(HEADS):
            mixed = att_scale * (att_acc[head(h), :] + nt(state[h], q[:, head(h)]))
            att[2 * h : 2 * h + 2] = mixed.astype(BF16).reshape(2, 2, 32, TOK)
        begin("attended", pair(att.at[:, 1 - core], att_in, 3))

    def terms_0():
        wait("out_grad")
        wait("attended")
        terms((0, 1))

    def terms_1():
        terms((2, 3))
        sent.append(lambda: scatter1_all(lambda copy: copy.wait_send()))

    def terms(turns):
        for turn in turns:
            a = (1 - core) * (turn // 2) + core * (turn % 2)
            half = (1 - core) * (turn % 2) + core * (turn // 2)
            blocks = pl.ds(a * NY + half * 4, 4)
            left = jnp.concatenate(
                [att[blocks, core].reshape(128, TOK), att_in[blocks].reshape(128, TOK)], 1
            )
            term = nn(left, g_both[...]).astype(BF16)
            for j in range(2):
                both = jnp.concatenate(
                    [
                        jnp.concatenate(
                            [term[b * 32 : b * 32 + 32, head(cb)] for cb in range(8)], 0
                        )
                        for b in (2 * j, 2 * j + 1)
                    ],
                    1,
                )
                units = nn(to_tiles[...], both).astype(BF16)
                for b in range(2):
                    sum1[:, :, a, half * 4 + 2 * j + b] = units[:, head(b)].reshape(NX, ZH, 16, 128)
            scatter1(turn)


    def att_grads():
        wait("gather3")
        place()
        wait("queries")
        for i in range(2):
            at = slice(i * 8, i * 8 + 8)
            grad = nt(weight[i * 256 : i * 256 + 256, :], g_both[...]).astype(BF16)
            att_grad[at, core] = grad[:, :TOK].reshape(8, 32, TOK)
            grad_give[at] = grad[:, TOK:].reshape(8, 32, TOK)
            for j in range(4):
                h, rows = i * 4 + j, slice(j * 64, j * 64 + 64)
                here = nn(grad[rows, :TOK], q[:, head(h)])
                there = nn(grad[rows, TOK:], q_other[:, head(h)])
                qd_own[2 * h : 2 * h + 2] = here.reshape(2, 32, HEAD)
                qd_other[2 * h : 2 * h + 2] = there.reshape(2, 32, HEAD)
                qd_out[2 * h : 2 * h + 2] = (here + there).astype(BF16).reshape(2, 32, HEAD)
        begin("qd there", exchange(qd_out, qd_in, 2))
        qd_in[chip] = qd_out[chip]
        for i in range(2):
            at = slice(i * 8, i * 8 + 8)
            begin(f"grad {i}", pair(grad_give.at[at], att_grad.at[at, core], 6 + i))

    def local_grads():
        wait("grad 0")
        wait("grad 1")
        for h in range(HEADS):
            grad = att_grad[2 * h : 2 * h + 2].reshape(HEAD, TOK)
            masked = jnp.where(causal_t, nn(v[:, head(h)], grad), 0.0).astype(BF16)
            dq_ref[:, head(h)] = (att_scale * (tn(masked, k[:, head(h)]) + tn(grad, state[h]))).astype(BF16)
            dk_acc[:, head(h)] = nn(masked, q[:, head(h)])
            dv_acc[:, head(h)] = nt(scores[h], grad)

    def second_scatter(part):
        def of_core_0():
            for half in range(2):
                for copy in scatter1_0(part, half):
                    copy.wait_recv()
            for far in range(ZH):
                value = sum1[x, far, part].astype(F32)
                for o in range(NX - 1):
                    value = value + in1[o, far, part].astype(F32)
                sum2[far * 2 + part] = value.astype(BF16)
                o = (far * 2 + part - z + NZ) % NZ

                @pl.when(o != 0)
                def _():
                    scatter2_z0(o).start()

        def of_core_1():
            rows = slice(part * 4, part * 4 + 4)
            for o in range(1, NZ):
                scatter1_z(o, part).wait_recv()
            value = sum1[0:2, zh, zl, rows].astype(F32)
            for o in range(NZ - 1):
                value = value + in1a[o, :, rows].astype(F32)
            sum2a[:, rows] = value.astype(BF16)
            for far in range(4):
                o = (part * 4 + far - y + NY) % NY

                @pl.when(o != 0)
                def _():
                    scatter2_y1(o).start()

            if part == 1:
                for o in range(1, NY):
                    scatter1_y(o).wait_recv()
                sum2b[...] = total_of(sum1[2:4, :, :, y], in1b).astype(BF16)
                for o in range(1, NZ):
                    scatter2_z1(o).start()

        by_core(of_core_0, of_core_1)
        if part == 1:
            open_waits["scatter2"] = lambda: scatter2_all(lambda copy: copy.wait_recv())
            sent.append(lambda: scatter2_all(lambda copy: copy.wait_send()))

    def second_scatter_0():
        second_scatter(0)

    def second_scatter_1():
        second_scatter(1)

    def qd_home():
        wait("qd there")
        running(qd_in, qd_sum, reversed(range(CHIPS)))
        begin("qd home", exchange(qd_sum, qd_back, 3))
        qd_back[chip] = qd_sum[chip]

    def third_scatter():
        wait("scatter2")

        def sum_0():
            sum3[...] = total_of(sum2[z], in2)

        def sum_1():
            sum3c[0:2] = total_of(sum2a[:, y], in2a)
            sum3c[2:4] = total_of(sum2b[:, zh, zl], in2b)

        by_core(sum_0, sum_1)
        begin_by_core("scatter3", scatter3_0, scatter3_1)

    def laters():
        wait("qd home")
        base = qd_back[...].astype(F32)
        carried[:, core] = jnp.where(core == 0, base + qd_other[...], base).astype(BF16)
        qd_give[...] = jnp.where(core == 0, base, base + qd_own[...]).astype(BF16)
        begin("carried", pair(qd_give, carried.at[:, core], 5))

    def weight_grad():
        wait("scatter3")

        def write(value):
            value = value * inv_root
            for row in range(2):
                for cb in range(8):
                    wg_ref[row : row + 1, head(cb)] = value[row * 8 + cb : row * 8 + cb + 1, :]

        by_core(lambda: write(total_of(sum3[y], in3)), lambda: write(total_of(sum3c[x], in3c)))

    def last_grads():
        wait("carried")
        for h in range(HEADS):
            later = carried[2 * h : 2 * h + 2].reshape(HEAD, HEAD)
            dk_ref[:, head(h)] = (att_scale * (dk_acc[:, head(h)] + nn(v[:, head(h)], later))).astype(BF16)
            dv_ref[:, head(h)] = (att_scale * (dv_acc[:, head(h)] + nt(k[:, head(h)], later))).astype(BF16)

    steps = [
        enter, begin_all, kv_there, second_gather, score, kv_home, third_gather, states,
        attend, terms_0, terms_1, att_grads, local_grads,
        second_scatter_0, second_scatter_1, qd_home, third_scatter, laters, weight_grad, last_grads,
    ]
    for step in steps:
        step()
    for name in list(open_waits):
        wait(name)
    for done in sent:
        done()


def store(*refs):
    sems = refs[8]
    copies = [pltpu.make_async_copy(refs[i], refs[4 + i], sems.at[i]) for i in range(4)]
    for copy in copies:
        copy.start()
    for copy in copies:
        copy.wait()


def per_device(queries, key_vecs, value_vecs, out_grad, out_weight):
    att_scale = 1.0 / math.sqrt(HEAD * TOK * NCTX)
    inv_root = 1.0 / math.sqrt(16 * TOK * NCTX)

    def body(*refs):
        kernel(att_scale, inv_root, *refs)

    hbm = pl.BlockSpec(memory_space=pltpu.HBM)
    vmem = pl.BlockSpec(memory_space=pltpu.VMEM)
    wide, narrow = pltpu.VMEM((TOK, D), F32), pltpu.VMEM((TOK, D), BF16)
    piece = pltpu.VMEM((CHIPS, 32, HEAD), BF16)
    scan = [
        pltpu.VMEM((HEADS, HEAD, HEAD), F32), pltpu.VMEM((HALF, HEAD, HEAD), F32),
        piece, piece, piece, piece,
        pltpu.VMEM((HALF, HEAD, HEAD), BF16), pltpu.VMEM((HEADS, HEAD, HEAD), BF16),
    ]
    unit = (16, 128)

    def units(*dims, kind=BF16):
        return pltpu.VMEM(dims + unit, kind)

    out = jax.ShapeDtypeStruct((TOK, D), BF16)
    dq, dk, dv, wg = pl.pallas_call(
        body,
        out_shape=(out, out, out, jax.ShapeDtypeStruct((2, D), F32)),
        in_specs=[hbm] * 5,
        out_specs=(vmem,) * 4,
        scratch_shapes=[
            narrow, narrow, narrow, pltpu.VMEM((2 * TOK, D), BF16), pltpu.VMEM((2, D), BF16), pltpu.VMEM((D, TOK), BF16), narrow,
            units(2, NY, 2, NX, ZH), pltpu.VMEM((D // 2, D), BF16), pltpu.VMEM(unit, F32),
            pltpu.VMEM((256, 256), BF16), pltpu.VMEM((256, 256), BF16),
            *scan,
            pltpu.VMEM((CHIPS, 32, HEAD), F32), pltpu.VMEM((CHIPS, 32, HEAD), F32),
            piece, piece, piece, piece, piece, pltpu.VMEM((CHIPS, 2, 32, HEAD), BF16),
            pltpu.VMEM((HEADS, TOK, TOK), BF16), pltpu.VMEM((D, TOK), F32),
            pltpu.VMEM((CHIPS, 2, 32, TOK), BF16), pltpu.VMEM((CHIPS, 32, TOK), BF16),
            pltpu.VMEM((CHIPS, 2, 32, TOK), BF16), pltpu.VMEM((CHIPS, 32, TOK), BF16), wide, wide,
            units(NX, ZH, 2, NY), units(NX - 1, ZH, 2, NY),
            units(NZ, NY), units(NZ - 1, NY), units(NY, kind=F32), units(NY - 1, kind=F32),
            units(NZ - 1, 2, NY), units(NY - 1, 2, ZH, 2), units(2, NY), units(2, ZH, 2),
            units(NY - 1, 2), units(NZ - 1, 2), units(NX, kind=F32), units(NX - 1, kind=F32),
            pltpu.SemaphoreType.DMA((5,)),
            pltpu.SemaphoreType.DMA((56,)), pltpu.SemaphoreType.DMA((56,)),
            pltpu.SemaphoreType.DMA((8,)), pltpu.SemaphoreType.DMA((8,)),
            pltpu.SemaphoreType.DMA((4, CHIPS)), pltpu.SemaphoreType.DMA((4, CHIPS)),
            pltpu.SemaphoreType.DMA((48,)), pltpu.SemaphoreType.DMA((48,)),
        ],
        compiler_params=pltpu.CompilerParams(
            collective_id=0, has_side_effects=True, vmem_limit_bytes=48 << 20
        ),
        name="backward",
    )(*(pltpu.with_memory_space_constraint(a, pltpu.HBM) for a in (queries[0], key_vecs[0], value_vecs[0], out_grad[0], out_weight)))
    dq, dk, dv, wg = pl.pallas_call(
        store,
        out_shape=(out, out, out, jax.ShapeDtypeStruct((2, D), F32)),
        in_specs=[vmem] * 4,
        out_specs=(hbm,) * 4,
        scratch_shapes=[pltpu.SemaphoreType.DMA((4,))],
        name="store",
    )(*(pltpu.with_memory_space_constraint(a, pltpu.VMEM) for a in (dq, dk, dv, wg)))
    return dq[None], dk[None], dv[None], wg


def solution(mesh):
    rows = P("dp", "ctx", None)
    return jax.shard_map(
        per_device,
        mesh=mesh,
        in_specs=(rows, rows, rows, rows, P(("ctx", "dp"), None)),
        out_specs=(rows, rows, rows, P(("ctx", "dp"), None)),
        check_vma=False,
    )
```

```python
import math

import jax
import jax.numpy as jnp
from jax import lax
from jax.experimental import pallas as pl
from jax.experimental.pallas import tpu as pltpu
from jax.sharding import PartitionSpec as P

HEAD = 128
HEADS = 8
HALF = HEADS // 2
TOK = 256
D = 1024
NX, NY, NZ = 4, 8, 8
ZH = NZ // 2
CHIPS = 2 * NY
NCTX = 2 * CHIPS
F32, BF16 = jnp.float32, jnp.bfloat16
MESH = pl.DeviceIdType.MESH


def device(x, y, z, core):
    return (((z % 2) * NY + y) * 2 + core, x * ZH + z // 2)


def dot(left, right, dims):
    return lax.dot_general(left, right, (dims, ((), ())), preferred_element_type=F32)


def tn(left, right):
    return dot(left, right, ((0,), (0,)))


def nt(left, right):
    return dot(left, right, ((1,), (1,)))


def nn(left, right):
    return dot(left, right, ((1,), (0,)))


def far_first(copies):
    n = len(copies) + 1
    if n == CHIPS:
        return [copies[o - 1] for o in sorted(range(1, n), key=lambda o: -min(o % NY, NY - o % NY))]
    if n == NY:
        return [copies[o - 1] for o in sorted(range(1, n), key=lambda o: -min(o, n - o))]
    return copies


def head(h):
    return slice(h * HEAD, h * HEAD + HEAD)


def kernel(
    att_scale, inv_root,
    q_hbm, k_hbm, v_hbm, g_hbm, w_hbm,
    dq_ref, dk_ref, dv_ref, wg_ref,
    q, k, v, g_both, w, v_turned, q_other,
    tiles, weight, flat, to_rows, to_tiles,
    kv, kv_pair, kv_out, kv_in, kv_sum, kv_back, kv_give, state,
    qd_own, qd_other, qd_out, qd_in, qd_sum, qd_back, qd_give, carried,
    scores, att_acc, att, att_in, att_grad, grad_give, dk_acc, dv_acc,
    sum1, in1, sum2, in2, sum3, in3,
    in1a, in1b, sum2a, sum2b, in2a, in2b, sum3c, in3c,
    load_sem, ag_s, ag_r, pair_s, pair_r, scan_s, scan_r, rs_s, rs_r,
):
    ctx, dp = lax.axis_index("ctx"), lax.axis_index("dp")
    core, chip = ctx % 2, ctx // 2
    y, zl = chip % NY, chip // NY
    x, zh = dp // ZH, dp % ZH
    z = zh * 2 + zl
    mine, theirs = pl.ds(core * HALF, HALF), pl.ds((1 - core) * HALF, HALF)
    other = (chip * 2 + 1 - core, dp)

    def at_x(o):
        return device((x + o) % NX, y, z, core)

    def at_y(o):
        return device(x, (y + o) % NY, z, core)

    def at_z(o):
        return device(x, y, (z + o) % NZ, core)

    def remote(src, dst, s, r, to):
        return pltpu.make_async_remote_copy(
            src_ref=src, dst_ref=dst, send_sem=s, recv_sem=r, device_id=to, device_id_type=MESH
        )

    def by_core(of_core_0, of_core_1):
        pl.when(core == 0)(of_core_0)
        pl.when(core == 1)(of_core_1)

    sent, open_waits = [], {}

    def begin(name, make):
        for copy in far_first(make()):
            copy.start()
        open_waits[name] = lambda: [copy.wait_recv() for copy in make()]
        sent.append(lambda: [copy.wait_send() for copy in make()])

    def begin_by_core(name, make_0, make_1):
        by_core(lambda: [copy.start() for copy in make_0()] and None, lambda: [copy.start() for copy in make_1()] and None)
        open_waits[name] = lambda: by_core(
            lambda: [copy.wait_recv() for copy in make_0()] and None,
            lambda: [copy.wait_recv() for copy in make_1()] and None,
        )
        sent.append(
            lambda: by_core(
                lambda: [copy.wait_send() for copy in make_0()] and None,
                lambda: [copy.wait_send() for copy in make_1()] and None,
            )
        )

    def wait(name):
        open_waits.pop(name)()

    g, g_other = g_both.at[0:TOK], g_both.at[TOK : 2 * TOK]

    loads = [
        pltpu.make_async_copy(src, dst, load_sem.at[i])
        for i, (src, dst) in enumerate(((w_hbm, w), (k_hbm, k), (v_hbm, v), (q_hbm, q), (g_hbm, g)))
    ]
    barrier = pltpu.get_barrier_semaphore()

    def enter():
        for load in loads:
            load.start()
        greeted = [((((chip + o) % CHIPS) * 2 + core), dp) for o in range(1, CHIPS)]
        greeted += [other]
        greeted += [at_x(o) for o in range(1, NX)]
        greeted += [
            device(x, y, (zh * 2 + 2 * (o // 2) + (zl + o) % 2) % NZ, core) for o in range(2, NZ)
        ]
        for to in greeted:
            pl.semaphore_signal(barrier, inc=1, device_id=to, device_id_type=MESH)
        loads[0].wait()
        own = w[...].astype(F32)
        for row in range(2):
            for cb in range(8):
                flat[row * 8 + cb : row * 8 + cb + 1, :] = own[row : row + 1, head(cb)]
        tiles[zl, y, core, x, zh] = flat[...].astype(BF16)
        pl.semaphore_wait(barrier, len(greeted))

    def products(which):
        for i in range(HALF):
            h = which * HALF + i
            cols = pl.ds(pl.multiple_of(h * HEAD, HEAD), HEAD)
            turned = v[:, cols].T
            v_turned[cols, :] = turned
            kv[h] = nn(turned, k[:, cols])

    def one_hot():
        rows_i = lax.broadcasted_iota(jnp.int32, (256, 256), 0)
        cols_i = lax.broadcasted_iota(jnp.int32, (256, 256), 1)

        def tile_row(i):
            return ((i & 31) >> 1) * 16 + (i & 1) * 8 + (i >> 5)

        to_rows[...] = jnp.where(cols_i == tile_row(rows_i), 1.0, 0.0).astype(BF16)
        to_tiles[...] = jnp.where(rows_i == tile_row(cols_i), 1.0, 0.0).astype(BF16)

    def ring(ref, first, to, n):
        return [remote(ref, ref, ag_s.at[first + o], ag_r.at[first + o], to(o)) for o in range(1, n)]

    def gather1_0():
        return ring(tiles.at[zl, y, 0, x, zh], 0, at_y, NY)

    def gather1_1():
        return ring(tiles.at[zl, y, 1, x, zh], 0, at_x, NX)

    def gather2_0():
        return ring(tiles.at[zl, :, 0, x, zh], 8, at_z, NZ)

    def gather2_1y():
        return ring(tiles.at[zl, y, 1, 0:2, zh], 8, at_y, NY)

    def gather2_1z():
        return ring(tiles.at[zl, y, 1, 2:4, zh], 16, at_z, NZ)

    def gather3_0(o):
        far = (z - o + NZ) % NZ
        return ring(tiles.at[far % 2, :, 0, x, far // 2], 24 + o * NX, at_x, NX)

    def gather3_1z():
        return ring(tiles.at[zl, :, 1, 0:2, zh], 24, at_z, NZ)

    def gather3_1y():
        return ring(tiles.at[:, y, 1, 2:4], 32, at_y, NY)

    def gather3_0_all():
        return [copy for o in range(NZ) for copy in gather3_0(o)]

    def start(copies):
        for copy in copies:
            copy.start()

    def second_gather():
        wait("gather1")

        def of_core_0():
            start(gather2_0())
            start(gather3_0(0))

        def of_core_1():
            start(gather2_1y())
            start(gather2_1z())

        by_core(of_core_0, of_core_1)

    def third_gather():
        def of_core_0():
            copies = gather2_0()
            for o in (1, 7, 2, 6, 3, 5, 4):
                copies[o - 1].wait_recv()
                start(gather3_0(o))

        def of_core_1():
            for copy in gather2_1y():
                copy.wait_recv()
            start(gather3_1z())
            for copy in gather2_1z():
                copy.wait_recv()
            start(gather3_1y())

        by_core(of_core_0, of_core_1)

        def all_of(last_only, act):
            def of_core_0():
                for copy in gather3_0_all() + ([] if last_only else gather2_0()):
                    act(copy)

            def of_core_1():
                for copy in gather3_1z() + gather3_1y() + ([] if last_only else gather2_1y() + gather2_1z()):
                    act(copy)

            by_core(of_core_0, of_core_1)

        open_waits["gather3"] = lambda: all_of(True, lambda copy: copy.wait_recv())
        sent.append(lambda: all_of(False, lambda copy: copy.wait_send()))

    def place():
        for b in range(NY):
            both = jnp.concatenate([tiles[a, b, core].reshape(256, 128) for a in range(2)], 1)
            rows = nn(to_rows[...], both).astype(BF16)
            for a in range(2):
                at = (a * NY + b) * 32
                for cb in range(8):
                    weight[at : at + 32, head(cb)] = rows[cb * 32 : cb * 32 + 32, head(a)]

    def pair(src, dst, i):
        return lambda: [remote(src, dst, pair_s.at[i], pair_r.at[i], other)]

    def exchange(src, dst, i):
        def make():
            copies = []
            for o in range(1, CHIPS):
                to = (chip + o) % CHIPS
                copies.append(
                    remote(src.at[to], dst.at[chip], scan_s.at[i, o], scan_r.at[i, o], (to * 2 + core, dp))
                )
            return copies

        return make

    def add_pair(product, received, out):
        for h in range(HALF):
            both = product[core * HALF + h] + received[h]
            out[h * 4 : h * 4 + 4] = both.astype(BF16).reshape(4, 32, HEAD)

    def running(received, out, order):
        total = jnp.zeros((32, HEAD), F32)
        for s in order:
            out[s] = total.astype(BF16)
            total = total + received[s].astype(F32)

    def finish():
        for h in range(HALF):
            base = kv_back[h * 4 : h * 4 + 4].reshape(HEAD, HEAD).astype(F32)
            state[core * HALF + h] = jnp.where(core == 1, base + kv_pair[h], base).astype(BF16)
            kv_give[h] = jnp.where(core == 1, base, base + kv[core * HALF + h]).astype(BF16)

    def spread(src, dst, first, to, n):
        return [remote(src(o), dst.at[o - 1], rs_s.at[first + o], rs_r.at[first + o], to(o)) for o in range(1, n)]

    def far_z(o):
        return (z + o) % NZ

    def far_y(o):
        return (y + o) % NY

    def scatter1_0(a, half):
        rows = pl.ds(half * 4, 4)
        copies = []
        for o in range(1, NX):
            i = (a * 2 + half) * NX + o
            copies.append(
                remote(
                    sum1.at[(x + o) % NX, :, a, rows], in1.at[o - 1, :, a, rows], rs_s.at[i], rs_r.at[i], at_x(o)
                )
            )
        return copies

    def scatter1_z(o, half):
        rows, far = pl.ds(half * 4, 4), (z + o) % NZ
        i = half * NZ + o
        return remote(
            sum1.at[0:2, far // 2, far % 2, rows], in1a.at[o - 1, :, rows], rs_s.at[i], rs_r.at[i], at_z(o)
        )

    def scatter1_y(o):
        i = 2 * NZ + o
        return remote(sum1.at[2:4, :, :, (y + o) % NY], in1b.at[o - 1], rs_s.at[i], rs_r.at[i], at_y(o))

    def scatter1(turn):
        def of_core_0():
            for copy in scatter1_0(turn // 2, turn % 2):
                copy.start()

        def of_core_1():
            a, half = turn % 2, turn // 2
            for far in range(ZH):
                o = (far * 2 + a - z + NZ) % NZ

                @pl.when(o != 0)
                def _():
                    scatter1_z(o, half).start()

            if a == 1:
                for far in range(4):
                    o = (half * 4 + far - y + NY) % NY

                    @pl.when(o != 0)
                    def _():
                        scatter1_y(o).start()

        by_core(of_core_0, of_core_1)

    def scatter1_all(act):
        def of_core_0():
            for half in range(2):
                for a in range(2):
                    for copy in scatter1_0(a, half):
                        act(copy)

        def of_core_1():
            for half in range(2):
                for o in range(1, NZ):
                    act(scatter1_z(o, half))
            for o in range(1, NY):
                act(scatter1_y(o))

        by_core(of_core_0, of_core_1)

    def scatter2_z0(o):
        far = (z + o) % NZ
        return remote(sum2.at[far], in2.at[o - 1], rs_s.at[24 + o], rs_r.at[24 + o], at_z(o))

    def scatter2_y1(o):
        far = (y + o) % NY
        return remote(sum2a.at[:, far], in2a.at[o - 1], rs_s.at[24 + o], rs_r.at[24 + o], at_y(o))

    def scatter2_z1(o):
        far = (z + o) % NZ
        return remote(
            sum2b.at[:, far // 2, far % 2], in2b.at[o - 1], rs_s.at[32 + o], rs_r.at[32 + o], at_z(o)
        )

    def scatter2_all(act):
        def of_core_0():
            for o in range(1, NZ):
                act(scatter2_z0(o))

        def of_core_1():
            for o in range(1, NY):
                act(scatter2_y1(o))
            for o in range(1, NZ):
                act(scatter2_z1(o))

        by_core(of_core_0, of_core_1)

    def scatter3_0():
        return spread(lambda o: sum3.at[far_y(o)], in3, 40, at_y, NY)

    def scatter3_1():
        return spread(lambda o: sum3c.at[(x + o) % NX], in3c, 40, at_x, NX)

    def total_of(own, received):
        value = own.astype(F32)
        for i in range(received.shape[0]):
            value = value + received[i].astype(F32)
        return value

    causal_t = lax.broadcasted_iota(jnp.int32, (TOK, TOK), 1) >= lax.broadcasted_iota(jnp.int32, (TOK, TOK), 0)

    def begin_all():
        begin_by_core("gather1", gather1_0, gather1_1)
        loads[1].wait()
        loads[2].wait()
        products(1 - core)
        begin("kv pair", pair(kv.at[theirs], kv_pair, 0))
        products(core)
        loads[3].wait()
        loads[4].wait()
        begin("out_grad", pair(g, g_other, 1))
        begin("queries", pair(q, q_other, 4))

    def kv_there():
        wait("kv pair")
        add_pair(kv, kv_pair, kv_out)
        begin("kv there", exchange(kv_out, kv_in, 0))
        kv_in[chip] = kv_out[chip]

    def score():
        for h in range(HEADS):
            masked = jnp.where(causal_t, nt(k[:, head(h)], q[:, head(h)]), 0.0).astype(BF16)
            scores[h] = masked
            att_acc[head(h), :] = nn(v_turned[head(h), :], masked)

    def kv_home():
        wait("kv there")
        running(kv_in, kv_sum, range(CHIPS))
        begin("kv home", exchange(kv_sum, kv_back, 1))
        kv_back[chip] = kv_sum[chip]
        one_hot()

    def states():
        wait("kv home")
        finish()
        begin("states", pair(kv_give, state.at[mine], 2))

    def attend():
        wait("states")
        for h in range(HEADS):
            mixed = att_scale * (att_acc[head(h), :] + nt(state[h], q[:, head(h)]))
            att[2 * h : 2 * h + 2] = mixed.astype(BF16).reshape(2, 2, 32, TOK)
        begin("attended", pair(att.at[:, 1 - core], att_in, 3))

    def terms_0():
        wait("out_grad")
        wait("attended")
        terms((0, 1))

    def terms_1():
        terms((2, 3))
        sent.append(lambda: scatter1_all(lambda copy: copy.wait_send()))

    def terms(turns):
        for turn in turns:
            a = (1 - core) * (turn // 2) + core * (turn % 2)
            half = (1 - core) * (turn % 2) + core * (turn // 2)
            blocks = pl.ds(a * NY + half * 4, 4)
            left = jnp.concatenate(
                [att[blocks, core].reshape(128, TOK), att_in[blocks].reshape(128, TOK)], 1
            )
            term = nn(left, g_both[...]).astype(BF16)
            for j in range(2):
                both = jnp.concatenate(
                    [
                        jnp.concatenate(
                            [term[b * 32 : b * 32 + 32, head(cb)] for cb in range(8)], 0
                        )
                        for b in (2 * j, 2 * j + 1)
                    ],
                    1,
                )
                units = nn(to_tiles[...], both).astype(BF16)
                for b in range(2):
                    sum1[:, :, a, half * 4 + 2 * j + b] = units[:, head(b)].reshape(NX, ZH, 16, 128)
            scatter1(turn)


    def att_grads():
        wait("gather3")
        place()
        wait("queries")
        for i in range(2):
            at = slice(i * 8, i * 8 + 8)
            grad = nt(weight[i * 256 : i * 256 + 256, :], g_both[...]).astype(BF16)
            att_grad[at, core] = grad[:, :TOK].reshape(8, 32, TOK)
            grad_give[at] = grad[:, TOK:].reshape(8, 32, TOK)
            for j in range(4):
                h, rows = i * 4 + j, slice(j * 64, j * 64 + 64)
                here = nn(grad[rows, :TOK], q[:, head(h)])
                there = nn(grad[rows, TOK:], q_other[:, head(h)])
                qd_own[2 * h : 2 * h + 2] = here.reshape(2, 32, HEAD)
                qd_other[2 * h : 2 * h + 2] = there.reshape(2, 32, HEAD)
                qd_out[2 * h : 2 * h + 2] = (here + there).astype(BF16).reshape(2, 32, HEAD)
        begin("qd there", exchange(qd_out, qd_in, 2))
        qd_in[chip] = qd_out[chip]
        for i in range(2):
            at = slice(i * 8, i * 8 + 8)
            begin(f"grad {i}", pair(grad_give.at[at], att_grad.at[at, core], 6 + i))

    def local_grads():
        wait("grad 0")
        wait("grad 1")
        for h in range(HEADS):
            grad = att_grad[2 * h : 2 * h + 2].reshape(HEAD, TOK)
            masked = jnp.where(causal_t, nn(v[:, head(h)], grad), 0.0).astype(BF16)
            dq_ref[:, head(h)] = (att_scale * (tn(masked, k[:, head(h)]) + tn(grad, state[h]))).astype(BF16)
            dk_acc[:, head(h)] = nn(masked, q[:, head(h)])
            dv_acc[:, head(h)] = nt(scores[h], grad)

    def second_scatter(part):
        def of_core_0():
            for half in range(2):
                for copy in scatter1_0(part, half):
                    copy.wait_recv()
            for far in range(ZH):
                value = sum1[x, far, part].astype(F32)
                for o in range(NX - 1):
                    value = value + in1[o, far, part].astype(F32)
                sum2[far * 2 + part] = value.astype(BF16)
                o = (far * 2 + part - z + NZ) % NZ

                @pl.when(o != 0)
                def _():
                    scatter2_z0(o).start()

        def of_core_1():
            rows = slice(part * 4, part * 4 + 4)
            for o in range(1, NZ):
                scatter1_z(o, part).wait_recv()
            value = sum1[0:2, zh, zl, rows].astype(F32)
            for o in range(NZ - 1):
                value = value + in1a[o, :, rows].astype(F32)
            sum2a[:, rows] = value.astype(BF16)
            for far in range(4):
                o = (part * 4 + far - y + NY) % NY

                @pl.when(o != 0)
                def _():
                    scatter2_y1(o).start()

            if part == 1:
                for o in range(1, NY):
                    scatter1_y(o).wait_recv()
                sum2b[...] = total_of(sum1[2:4, :, :, y], in1b).astype(BF16)
                for o in range(1, NZ):
                    scatter2_z1(o).start()

        by_core(of_core_0, of_core_1)
        if part == 1:
            open_waits["scatter2"] = lambda: scatter2_all(lambda copy: copy.wait_recv())
            sent.append(lambda: scatter2_all(lambda copy: copy.wait_send()))

    def second_scatter_0():
        second_scatter(0)

    def second_scatter_1():
        second_scatter(1)

    def qd_home():
        wait("qd there")
        running(qd_in, qd_sum, reversed(range(CHIPS)))
        begin("qd home", exchange(qd_sum, qd_back, 3))
        qd_back[chip] = qd_sum[chip]

    def third_scatter():
        wait("scatter2")

        def sum_0():
            sum3[...] = total_of(sum2[z], in2)

        def sum_1():
            sum3c[0:2] = total_of(sum2a[:, y], in2a)
            sum3c[2:4] = total_of(sum2b[:, zh, zl], in2b)

        by_core(sum_0, sum_1)
        begin_by_core("scatter3", scatter3_0, scatter3_1)

    def laters():
        wait("qd home")
        base = qd_back[...].astype(F32)
        carried[:, core] = jnp.where(core == 0, base + qd_other[...], base).astype(BF16)
        qd_give[...] = jnp.where(core == 0, base, base + qd_own[...]).astype(BF16)
        begin("carried", pair(qd_give, carried.at[:, core], 5))

    def weight_grad():
        wait("scatter3")

        def write(value):
            value = value * inv_root
            for row in range(2):
                for cb in range(8):
                    wg_ref[row : row + 1, head(cb)] = value[row * 8 + cb : row * 8 + cb + 1, :]

        by_core(lambda: write(total_of(sum3[y], in3)), lambda: write(total_of(sum3c[x], in3c)))

    def last_grads():
        wait("carried")
        for h in range(HEADS):
            later = carried[2 * h : 2 * h + 2].reshape(HEAD, HEAD)
            dk_ref[:, head(h)] = (att_scale * (dk_acc[:, head(h)] + nn(v[:, head(h)], later))).astype(BF16)
            dv_ref[:, head(h)] = (att_scale * (dv_acc[:, head(h)] + nt(k[:, head(h)], later))).astype(BF16)

    steps = [
        enter, begin_all, kv_there, second_gather, score, kv_home, third_gather, states,
        attend, terms_0, terms_1, att_grads, local_grads,
        second_scatter_0, second_scatter_1, qd_home, third_scatter, laters, weight_grad, last_grads,
    ]
    for step in steps:
        step()
    for name in list(open_waits):
        wait(name)
    for done in sent:
        done()


def store(*refs):
    sems = refs[8]
    copies = [pltpu.make_async_copy(refs[i], refs[4 + i], sems.at[i]) for i in range(4)]
    for copy in copies:
        copy.start()
    for copy in copies:
        copy.wait()


def per_device(queries, key_vecs, value_vecs, out_grad, out_weight):
    att_scale = 1.0 / math.sqrt(HEAD * TOK * NCTX)
    inv_root = 1.0 / math.sqrt(16 * TOK * NCTX)

    def body(*refs):
        kernel(att_scale, inv_root, *refs)

    hbm = pl.BlockSpec(memory_space=pltpu.HBM)
    vmem = pl.BlockSpec(memory_space=pltpu.VMEM)
    wide, narrow = pltpu.VMEM((TOK, D), F32), pltpu.VMEM((TOK, D), BF16)
    piece = pltpu.VMEM((CHIPS, 32, HEAD), BF16)
    scan = [
        pltpu.VMEM((HEADS, HEAD, HEAD), F32), pltpu.VMEM((HALF, HEAD, HEAD), F32),
        piece, piece, piece, piece,
        pltpu.VMEM((HALF, HEAD, HEAD), BF16), pltpu.VMEM((HEADS, HEAD, HEAD), BF16),
    ]
    unit = (16, 128)

    def units(*dims, kind=BF16):
        return pltpu.VMEM(dims + unit, kind)

    out = jax.ShapeDtypeStruct((TOK, D), BF16)
    dq, dk, dv, wg = pl.pallas_call(
        body,
        out_shape=(out, out, out, jax.ShapeDtypeStruct((2, D), F32)),
        in_specs=[hbm] * 5,
        out_specs=(vmem,) * 4,
        scratch_shapes=[
            narrow, narrow, narrow, pltpu.VMEM((2 * TOK, D), BF16), pltpu.VMEM((2, D), BF16), pltpu.VMEM((D, TOK), BF16), narrow,
            units(2, NY, 2, NX, ZH), pltpu.VMEM((D // 2, D), BF16), pltpu.VMEM(unit, F32),
            pltpu.VMEM((256, 256), BF16), pltpu.VMEM((256, 256), BF16),
            *scan,
            pltpu.VMEM((CHIPS, 32, HEAD), F32), pltpu.VMEM((CHIPS, 32, HEAD), F32),
            piece, piece, piece, piece, piece, pltpu.VMEM((CHIPS, 2, 32, HEAD), BF16),
            pltpu.VMEM((HEADS, TOK, TOK), BF16), pltpu.VMEM((D, TOK), F32),
            pltpu.VMEM((CHIPS, 2, 32, TOK), BF16), pltpu.VMEM((CHIPS, 32, TOK), BF16),
            pltpu.VMEM((CHIPS, 2, 32, TOK), BF16), pltpu.VMEM((CHIPS, 32, TOK), BF16), wide, wide,
            units(NX, ZH, 2, NY), units(NX - 1, ZH, 2, NY),
            units(NZ, NY), units(NZ - 1, NY), units(NY, kind=F32), units(NY - 1, kind=F32),
            units(NZ - 1, 2, NY), units(NY - 1, 2, ZH, 2), units(2, NY), units(2, ZH, 2),
            units(NY - 1, 2), units(NZ - 1, 2), units(NX, kind=F32), units(NX - 1, kind=F32),
            pltpu.SemaphoreType.DMA((5,)),
            pltpu.SemaphoreType.DMA((56,)), pltpu.SemaphoreType.DMA((56,)),
            pltpu.SemaphoreType.DMA((8,)), pltpu.SemaphoreType.DMA((8,)),
            pltpu.SemaphoreType.DMA((4, CHIPS)), pltpu.SemaphoreType.DMA((4, CHIPS)),
            pltpu.SemaphoreType.DMA((48,)), pltpu.SemaphoreType.DMA((48,)),
        ],
        compiler_params=pltpu.CompilerParams(
            collective_id=0, has_side_effects=True, vmem_limit_bytes=48 << 20
        ),
        name="backward",
    )(*(pltpu.with_memory_space_constraint(a, pltpu.HBM) for a in (queries[0], key_vecs[0], value_vecs[0], out_grad[0], out_weight)))
    dq, dk, dv, wg = pl.pallas_call(
        store,
        out_shape=(out, out, out, jax.ShapeDtypeStruct((2, D), F32)),
        in_specs=[vmem] * 4,
        out_specs=(hbm,) * 4,
        scratch_shapes=[pltpu.SemaphoreType.DMA((4,))],
        name="store",
    )(*(pltpu.with_memory_space_constraint(a, pltpu.VMEM) for a in (dq, dk, dv, wg)))
    return dq[None], dk[None], dv[None], wg


def solution(mesh):
    rows = P("dp", "ctx", None)
    return jax.shard_map(
        per_device,
        mesh=mesh,
        in_specs=(rows, rows, rows, rows, P(("ctx", "dp"), None)),
        out_specs=(rows, rows, rows, P(("ctx", "dp"), None)),
        check_vma=False,
    )
```
